512 devices in a mesh: scan: 128 (over z, y, core), mode: 4 (over x).
Axes of the slice: x: 4, y: 8, z: 8, core: 2. Of those that a mesh axis runs over, the one named last changes fastest.
Arguments:
- object_field: float32 [2, 8192, 1024], P(None, 'scan', 'mode'), may hold values from -6 to 6
- probe: float32 [4, 2, 128, 128], P('mode'), may hold values from -6 to 6
- amplitude: float32 [1024, 128, 128], P(('scan', 'mode')), may hold values from 0.5 to 8
- offsets: int32 [1024, 2], P(('scan', 'mode')), may hold values from 0 to 8191, as said below
- counts: int32 [512], P(('scan', 'mode')), may hold values from 1 to 2, as said below
Outputs:
- object_out: float32 [2, 8192, 1024], P(None, 'scan', 'mode')
- probe_out: float32 [4, 2, 128, 128], P('mode')
The draws below stay inside these ranges and needn't reach their ends.
Inputs may be any that keep to these rules, and one draw needn't show every extreme that they name: `offsets`: slot i belongs to the device of index i // 2 along scan+mode, with scan index s and mode index m; its top row lies in s * 64 to s * 64 + 63 and its left column in m * 256 to m * 256 + 255. `counts`: entry d is how many of the first slots of device d are used; some device uses all 2.
All inputs are finite; a program needn't handle non-finite values.
Results may differ from the reference program's by a relative error of at most 0.0001.
Values sent between devices are 32-bit elements; how exact they have to be, the bound alone decides.
A program may use at most 64 MiB of HBM per device.

```python
import math
import jax
import jax.numpy as jnp
from jax import lax

P_SIZE = 128
TR = 64
BW = 256
POS_DEV = 2
ITERS = 2
MODES = 4
NO = 8192
NC = 1024
NPOS = 1024


def draw_offsets(key, part):
    key_row, key_col = jax.random.split(jax.random.fold_in(key, 11))
    slot_ids = jnp.arange(NPOS, dtype=jnp.int32)
    device_ids = slot_ids // POS_DEV
    band_count = NC // BW
    tile_ids = device_ids // band_count
    band_ids = device_ids % band_count
    row_start = tile_ids * TR + jax.random.randint(key_row, (NPOS,), 0, TR, dtype=jnp.int32)
    col_start = band_ids * BW + jax.random.randint(key_col, (NPOS,), 0, BW, dtype=jnp.int32)
    row_start = jnp.where(slot_ids == NPOS - 1, NO - 1, row_start)
    col_start = jnp.where(slot_ids == NPOS - 1, NC - 1, col_start)
    row_start = jnp.where(slot_ids == 0, 0, row_start)
    col_start = jnp.where(slot_ids == 0, 0, col_start)
    return jnp.stack([row_start, col_start], axis=1)


def draw_counts(key, part):
    key_count, key_full = jax.random.split(jax.random.fold_in(key, 23))
    group_total = NPOS // POS_DEV
    counts_drawn = jax.random.randint(key_count, (group_total,), 1, POS_DEV + 1, dtype=jnp.int32)
    chosen = jax.random.randint(key_full, (), 0, group_total, dtype=jnp.int32)
    return jnp.where(jnp.arange(group_total, dtype=jnp.int32) == chosen, POS_DEV, counts_drawn)


def levels(stream_key, dims, cuts, low, largest):
    gain = 1.0
    for axis_at, shards_of in cuts:
        heights = jax.random.uniform(jax.random.fold_in(jax.random.fold_in(stream_key, 6), axis_at), (shards_of,), jnp.float32, low / len(cuts), largest / len(cuts))
        gain = gain * jnp.repeat(jnp.exp(heights), dims[axis_at] // shards_of).reshape((-1,) + (1,) * (len(dims) - 1 - axis_at))
    return gain


def normal_values(stream_key, extent, deviation, bound, pieces=(), kind=jnp.bfloat16):
    drawn = jax.random.normal(stream_key, extent, jnp.float32) * deviation
    if len(pieces) > 0:
        drawn = levels(stream_key, extent, pieces, -0.22, 0.18) * drawn
    return jnp.clip(drawn, min=-bound, max=bound).astype(kind)


def setup_inputs(seed: int = 0) -> dict:
    key_of = jax.random.split(jax.random.key(seed), 6)
    return {
        "object_field": normal_values(key_of[0], (2, NO, NC), 1.0, 6.0, ((1, 128), (2, 4)), jnp.float32),
        "probe": normal_values(key_of[1], (MODES, 2, P_SIZE, P_SIZE), 1.0, 6.0, ((0, 4),), jnp.float32),
        "amplitude": jnp.clip(jnp.exp(math.log(8.0) - 2.7725887 * jax.random.uniform(key_of[2], (NPOS, P_SIZE, P_SIZE), jnp.float32) ** levels(key_of[2], (NPOS, P_SIZE, P_SIZE), ((0, 512),), -0.2, 0.2)), 0.5, 8.0),
        "offsets": draw_offsets(jax.random.fold_in(key_of[5], 71), 0),
        "counts": draw_counts(jax.random.fold_in(key_of[5], 71), 0),
    }


def fresnel_table(length):
    pixel_ids = jnp.arange(length, dtype=jnp.int32)
    phase_grid = pixel_ids[:, None] * pixel_ids[None, :] % length
    centred = pixel_ids - length // 2
    chirp = centred * centred % (4 * length)
    angle_table = -2.0 * math.pi / length * phase_grid.astype(jnp.float32) + math.pi / (2 * length) * chirp[None, :].astype(jnp.float32)
    factor = 1.0 / math.sqrt(length)
    return (jnp.cos(angle_table) * factor, jnp.sin(angle_table) * factor)

def product(form, first, second):
    return jnp.einsum(form, first, second, precision=lax.Precision.HIGHEST)

def wave_terms(object_patch, probes, amplitude_row, kern_re, kern_im):
    probe_re = probes[:, 0]
    probe_im = probes[:, 1]
    object_re = object_patch[0]
    object_im = object_patch[1]
    exit_re = probe_re * object_re - probe_im * object_im
    exit_im = probe_re * object_im + probe_im * object_re
    left_re = product('ux,kxy->kuy', kern_re, exit_re) - product('ux,kxy->kuy', kern_im, exit_im)
    left_im = product('ux,kxy->kuy', kern_re, exit_im) + product('ux,kxy->kuy', kern_im, exit_re)
    far_re = product('kuy,vy->kuv', left_re, kern_re) - product('kuy,vy->kuv', left_im, kern_im)
    far_im = product('kuy,vy->kuv', left_re, kern_im) + product('kuy,vy->kuv', left_im, kern_re)
    intensity = lax.optimization_barrier(jnp.sum(far_re * far_re + far_im * far_im, axis=0))
    factor = amplitude_row / jnp.sqrt(jnp.maximum(intensity, 1.0))
    fixed_re = far_re * factor
    fixed_im = far_im * factor
    back_re = product('ux,kuy->kxy', kern_re, fixed_re) + product('ux,kuy->kxy', kern_im, fixed_im)
    back_im = product('ux,kuy->kxy', kern_re, fixed_im) - product('ux,kuy->kxy', kern_im, fixed_re)
    near_re = product('kxv,vy->kxy', back_re, kern_re) + product('kxv,vy->kxy', back_im, kern_im)
    near_im = product('kxv,vy->kxy', back_im, kern_re) - product('kxv,vy->kxy', back_re, kern_im)
    change_re = near_re - exit_re
    change_im = near_im - exit_im
    numerator = jnp.stack([lax.optimization_barrier(jnp.sum(probe_re * change_re + probe_im * change_im, axis=0)), lax.optimization_barrier(jnp.sum(probe_re * change_im - probe_im * change_re, axis=0)), lax.optimization_barrier(jnp.sum(probe_re * probe_re + probe_im * probe_im, axis=0))])
    gradient = jnp.stack([object_re * change_re + object_im * change_im, object_re * change_im - object_im * change_re], axis=1)
    density = object_re * object_re + object_im * object_im
    return (numerator, gradient, density)

def reference(object_field, probe, amplitude, offsets, counts):
    kern_re, kern_im = fresnel_table(P_SIZE)
    slot_ids = jnp.arange(NPOS, dtype=jnp.int32)
    used_all = (slot_ids % POS_DEV < counts[slot_ids // POS_DEV]).astype(jnp.float32)
    start_zero = jnp.zeros((), jnp.int32)
    for iteration in range(ITERS):
        padded = jnp.pad(object_field, ((0, 0), (0, P_SIZE), (0, P_SIZE)))

        def add_position(slot, state_carry):
            sums, gradient, density = state_carry
            row_start = offsets[slot, 0].astype(jnp.int32)
            col_start = offsets[slot, 1].astype(jnp.int32)
            object_patch = lax.dynamic_slice(padded, (start_zero, row_start, col_start), (2, P_SIZE, P_SIZE))
            numerator, grad_term, dens_term = wave_terms(object_patch, probe, amplitude[slot], kern_re, kern_im)
            used = used_all[slot]
            current = lax.dynamic_slice(sums, (start_zero, row_start, col_start), (3, P_SIZE, P_SIZE))
            sums = lax.dynamic_update_slice(sums, current + used * numerator, (start_zero, row_start, col_start))
            return (sums, gradient + used * grad_term, density + used * dens_term)
        initial = (jnp.zeros((3, NO + P_SIZE, NC + P_SIZE), jnp.float32), jnp.zeros(probe.shape, jnp.float32), jnp.zeros((P_SIZE, P_SIZE), jnp.float32))
        sums, gradient, density = lax.fori_loop(0, NPOS, add_position, initial)
        object_new = object_field + sums[:2, :NO, :NC] / (sums[2:3, :NO, :NC] + 1.0)
        probe = probe + gradient / (density + 1.0)
        object_field = object_new
    return (object_field, probe)
```

```python
import math

import jax
import jax.numpy as jnp
import ml_dtypes
import numpy as np
from jax import lax
from jax.experimental import pallas as pl
from jax.experimental.pallas import tpu as pltpu
from jax.sharding import PartitionSpec as P

ITERS = 2
CORES = 2
N = 128
MESH = pl.DeviceIdType.MESH
F32 = jnp.float32
BF16 = jnp.bfloat16


def fresnel_blocks():
    ids = np.arange(N)
    phase = (ids[:, None] * ids[None, :]) % N
    chirp = ((ids - N // 2) ** 2) % (4 * N)
    angle = -2.0 * math.pi / N * phase + math.pi / (2 * N) * chirp[None, :]
    re, im = np.cos(angle) / math.sqrt(N), np.sin(angle) / math.sqrt(N)
    full = np.block([[re, -im], [im, re]]).astype(np.float32)

    def parts(matrix):
        high = matrix.astype(ml_dtypes.bfloat16)
        low = (matrix - high.astype(np.float32)).astype(ml_dtypes.bfloat16)
        return np.stack([high, low])

    return parts(full), parts(np.ascontiguousarray(full.T))


def split(value):
    high = value.astype(BF16)
    return high, (value - high.astype(F32)).astype(BF16)


def dot(first, second):
    return jnp.dot(first, second, preferred_element_type=F32)


def dot3(first_high, first_low, second_high, second_low):
    return dot(first_high, second_high) + dot(first_high, second_low) + dot(first_low, second_high)


class Plan:
    def __init__(self, n_scan, n_mode, tile_rows):
        self.n_scan, self.n_mode, self.tile = n_scan, n_mode, tile_rows
        self.side = math.isqrt(n_scan // CORES)
        assert self.side * self.side * CORES == n_scan
        self.planes = 2 * n_mode
        self.half = N // CORES
        self.rows = self.half // self.side
        self.own_planes = self.planes // self.side


def make_kernel(plan):
    n_scan, n_mode, tile, side = plan.n_scan, plan.n_mode, plan.tile, plan.side
    planes, half, rows, own_planes = plan.planes, plan.half, plan.rows, plan.own_planes
    far_rows = n_scan * tile
    far_cols = n_mode * 2 * N

    def kernel(
        obj_ref, probe_ref, amp_ref, left_ref, right_ref, off_ref, cnt_ref,
        obj_out, probe_out,
        ext, probes, sums, pad, patch, exits, ah, al, xh, xl,
        grad, land_core, acc_core, land_row, acc_row, land_plane, land_x, tail,
        land_a, land_b,
        s_probe, r_probe, s_fwd, r_fwd, s_halo, r_halo, s_sum, r_sum,
        s_core, r_core, s_row, r_row, s_plane, r_plane, s_x, r_x,
        s_gp, r_gp, s_gr, r_gr, s_gc, r_gc,
    ):
        s = lax.axis_index("scan")
        m = lax.axis_index("mode")
        core = lax.rem(s, CORES)
        chip = lax.div(s, CORES)
        y, z = lax.rem(chip, side), lax.div(chip, side)
        a = y * (1 - core) + z * core
        b = z * (1 - core) + y * core

        def at(first, second):
            yy = first * (1 - core) + second * core
            zz = second * (1 - core) + first * core
            return ((zz * side + yy) * CORES + core, m)

        other = (s + 1 - 2 * core, m)

        def near(ds, dm):
            return (lax.rem(s + ds + n_scan, n_scan), lax.rem(m + dm + n_mode, n_mode))

        peers_a = [(lax.rem(a + d, side), at(lax.rem(a + d, side), b)) for d in range(1, side)]
        peers_b = [(lax.rem(b + d, side), at(a, lax.rem(b + d, side))) for d in range(1, side)]
        peers_x = [near(0, d) for d in range(1, n_mode)]
        halo_steps = [(1, 0), (2, 0), (0, 1), (1, 1), (2, 1)]
        before = [near(-ds, -dm) for ds, dm in halo_steps]
        after = [near(ds, dm) for ds, dm in halo_steps]
        peers = [other] + [p for _, p in peers_a] + [p for _, p in peers_b] + peers_x + before + after

        started = []

        def send(src, dst, send_sem, recv_sem, device):
            copy = pltpu.make_async_remote_copy(
                src_ref=src, dst_ref=dst, send_sem=send_sem, recv_sem=recv_sem,
                device_id=device, device_id_type=MESH,
            )
            copy.start()
            started.append(copy)
            return copy

        barrier = pltpu.get_barrier_semaphore()
        for device in peers:
            pl.semaphore_signal(barrier, inc=1, device_id=device, device_id_type=MESH)

        for c in range(2):
            ext[0, :, c, 0:tile, :] = obj_ref[:, :, c * N : (c + 1) * N]
        probes[0, pl.ds(2 * m, 2)] = probe_ref[0]
        zero_half = jnp.zeros((64, N), F32)
        zero_block = jnp.zeros((256, N), F32)
        for p in range(3):
            pad[p, 0] = zero_block
            pad[p, 3] = zero_block
            for c in (1, 2):
                pad[p, c, 0:64, :] = zero_half
                pad[p, c, 192:256, :] = zero_half

        pl.semaphore_wait(barrier, len(peers))

        def start_halo(it):
            copies = []
            for i in (1, 2):
                copies.append(
                    send(ext.at[it, :, pl.ds(0, 2), pl.ds(0, tile), :],
                         ext.at[it, :, pl.ds(0, 2), pl.ds(i * tile, tile), :],
                         s_halo.at[it, i - 1], r_halo.at[it, i - 1], before[i - 1])
                )
            for i in range(3):
                copies.append(
                    send(ext.at[it, :, 0, pl.ds(0, tile), :],
                         ext.at[it, :, 2, pl.ds(i * tile, tile), :],
                         s_halo.at[it, 2 + i], r_halo.at[it, 2 + i], before[2 + i])
                )
            return copies

        mine = pl.ds(core * half, half)
        own_mode = pl.ds(2 * m, 2)
        probe_copies = [
            send(probes.at[0, own_mode, mine, :], probes.at[0, own_mode, mine, :],
                 s_probe.at[d - 1], r_probe.at[d - 1], peers_x[d - 1])
            for d in range(1, n_mode)
        ]
        halo_copies = start_halo(0)
        forwards = []
        for d in range(1, n_mode):
            probe_copies[d - 1].wait_recv()
            came = pl.ds(2 * lax.rem(m - d + n_mode, n_mode), 2)
            forwards.append(
                send(probes.at[0, came, mine, :], probes.at[0, came, mine, :],
                     s_fwd.at[d - 1], r_fwd.at[d - 1], other)
            )
        for copy in forwards:
            copy.wait_recv()

        lane = lax.broadcasted_iota(jnp.int32, (N, N), 1)
        row_id = lax.broadcasted_iota(jnp.int32, (N, N), 0)

        def position(it, j):
            top, leftmost = off_ref[j, 0], off_ref[j, 1]
            row, col = lax.rem(top, tile), lax.rem(leftmost, 2 * N)
            col_block, col_lane = lax.div(col, N), lax.rem(col, N)
            used = jnp.where(j < cnt_ref[0], 1.0, 0.0).astype(F32)
            back_shift = lax.rem(N - col_lane, N)
            inside = (row_id + top < far_rows) & (lane + leftmost < far_cols)
            for p in range(2):
                one = ext[it, p, col_block, pl.ds(row, N), :]
                two = ext[it, p, col_block + 1, pl.ds(row, N), :]
                moved = pltpu.roll(jnp.where(lane >= col_lane, one, two), back_shift, 1)
                patch[p] = jnp.where(inside, moved, 0.0)
            for k in range(n_mode):
                spot = pl.ds(k * N, N)
                pr, pi = probes[it, 2 * k], probes[it, 2 * k + 1]
                o_re, o_im = patch[0], patch[1]
                e_re = pr * o_re - pi * o_im
                e_im = pr * o_im + pi * o_re
                for c, value in ((0, e_re), (1, e_im)):
                    where_c = pl.ds(c * N, N)
                    exits[spot, where_c] = value
                    high, low = split(value)
                    ah[spot, where_c] = high
                    al[spot, where_c] = low
            mid = dot3(ah[...], al[...], right_ref[0], right_ref[1])
            high, low = split(mid)
            for k in range(n_mode):
                for c in range(2):
                    block = (slice(k * N, (k + 1) * N), slice(c * N, (c + 1) * N))
                    turned = (pl.ds(c * N, N), pl.ds(k * N, N))
                    xh[turned] = high[block]
                    xl[turned] = low[block]
            far = dot3(left_ref[0], left_ref[1], xh[...], xl[...])
            intensity = jnp.zeros((N, N), F32)
            for k in range(n_mode):
                for c in range(2):
                    part = far[c * N : (c + 1) * N, k * N : (k + 1) * N]
                    intensity = intensity + part * part
            factor = amp_ref[j] / jnp.sqrt(jnp.maximum(intensity, 1.0))
            for k in range(n_mode):
                for c in range(2):
                    part = far[c * N : (c + 1) * N, k * N : (k + 1) * N] * factor
                    high, low = split(part)
                    xh[pl.ds(c * N, N), pl.ds(k * N, N)] = high
                    xl[pl.ds(c * N, N), pl.ds(k * N, N)] = low
            back = dot3(right_ref[0], right_ref[1], xh[...], xl[...])
            high, low = split(back)
            for k in range(n_mode):
                for c in range(2):
                    block = (slice(c * N, (c + 1) * N), slice(k * N, (k + 1) * N))
                    turned = (pl.ds(k * N, N), pl.ds(c * N, N))
                    ah[turned] = high[block]
                    al[turned] = low[block]
            near_field = dot3(ah[...], al[...], left_ref[0], left_ref[1])
            exits[...] = near_field - exits[...]
            num_re = jnp.zeros((N, N), F32)
            num_im = jnp.zeros((N, N), F32)
            weight = jnp.zeros((N, N), F32)
            o_re, o_im = patch[0] * used, patch[1] * used
            for k in range(n_mode):
                spot = pl.ds(k * N, N)
                c_re, c_im = exits[spot, pl.ds(0, N)], exits[spot, pl.ds(N, N)]
                pr, pi = probes[it, 2 * k], probes[it, 2 * k + 1]
                num_re = num_re + (pr * c_re + pi * c_im)
                num_im = num_im + (pr * c_im - pi * c_re)
                weight = weight + (pr * pr + pi * pi)
                g_re = o_re * c_re + o_im * c_im
                g_im = o_re * c_im - o_im * c_re
                if j == 0:
                    grad[it, 2 * k] = g_re
                    grad[it, 2 * k + 1] = g_im
                else:
                    grad[it, 2 * k] += g_re
                    grad[it, 2 * k + 1] += g_im
            density = o_re * patch[0] + o_im * patch[1]
            if j == 0:
                grad[it, planes] = density
            else:
                grad[it, planes] += density
            for p, value in enumerate((num_re, num_im, weight)):
                moved = pltpu.roll(value * used, col_lane, 1)
                pad[p, 1, 64:192, :] = jnp.where(lane >= col_lane, moved, 0.0)
                pad[p, 2, 64:192, :] = jnp.where(lane < col_lane, moved, 0.0)
            for p in range(3):
                for c in range(3):
                    placed = pad[p, c + 1 - col_block, pl.ds(64 - row, 192), :]
                    if j == 0:
                        sums[it, p, c] = placed
                    else:
                        sums[it, p, c] += placed

        def reduce_steps(it):
            last = it == ITERS - 1
            theirs = pl.ds((1 - core) * half, half)
            copy = send(grad.at[it, :, theirs, :], land_core.at[it], s_core.at[it], r_core.at[it], other)
            yield
            copy.wait_recv()
            acc_core[it] = grad[it, :, mine, :] + land_core[it]
            copies = [
                send(acc_core.at[it, :, pl.ds(pl.multiple_of(t * rows, rows), rows), :], land_row.at[it, i],
                     s_row.at[it, i], r_row.at[it, i], device)
                for i, (t, device) in enumerate(peers_a)
            ]
            yield
            total = acc_core[it, :, pl.ds(pl.multiple_of(a * rows, rows), rows), :]
            for i, copy in enumerate(copies):
                copy.wait_recv()
                total = total + land_row[it, i]
            for t in range(side):
                acc_row[it, t, 0:own_planes] = total[t * own_planes : (t + 1) * own_planes]
                acc_row[it, t, own_planes] = total[planes]
            copies = [
                send(acc_row.at[it, t], land_plane.at[it, i], s_plane.at[it, i], r_plane.at[it, i], device)
                for i, (t, device) in enumerate(peers_b)
            ]
            yield
            total = acc_row[it, b]
            for i, copy in enumerate(copies):
                copy.wait_recv()
                total = total + land_plane[it, i]
            land_x[it, m] = total
            copies = [
                send(land_x.at[it, m], land_x.at[it, m], s_x.at[it, i], r_x.at[it, i], device)
                for i, device in enumerate(peers_x)
            ]
            yield
            for copy in copies:
                copy.wait_recv()
            total = land_x[it, 0]
            for i in range(1, n_mode):
                total = total + land_x[it, i]
            first_row = pl.multiple_of(core * half + a * rows, rows)
            spot = pl.ds(first_row, rows)
            own = pl.ds(b * own_planes, own_planes)
            fresh = probes[it, own, spot, :] + total[0:own_planes] / (total[own_planes : own_planes + 1] + 1.0)
            probes[it + 1, own, spot, :] = fresh
            piece = probes.at[it + 1, own, spot, :]
            copies = [
                send(piece, piece, s_gp.at[it, i], r_gp.at[it, i], device) for i, (t, device) in enumerate(peers_b)
            ]
            yield
            for copy in copies:
                copy.wait_recv()
            kept = own_mode if last else pl.ds(0, planes)
            piece = probes.at[it + 1, kept, spot, :]
            copies = [
                send(piece, piece, s_gr.at[it, i], r_gr.at[it, i], device) for i, (t, device) in enumerate(peers_a)
            ]
            yield
            for copy in copies:
                copy.wait_recv()
            piece = probes.at[it + 1, kept, mine, :]
            copy = send(piece, piece, s_gc.at[it], r_gc.at[it], other)
            yield
            copy.wait_recv()

        def start_sums(it):
            copies = []
            for i in (1, 2):
                copies.append(
                    send(sums.at[it, :, pl.ds(0, 2), pl.ds(i * tile, tile), :], land_a.at[it, i - 1],
                         s_sum.at[it, i - 1], r_sum.at[it, i - 1], after[i - 1])
                )
            for i in range(3):
                copies.append(
                    send(sums.at[it, :, 2, pl.ds(i * tile, tile), :], land_b.at[it, i],
                         s_sum.at[it, 2 + i], r_sum.at[it, 2 + i], after[2 + i])
                )
            return copies

        def finish_sums(it, copies):
            for copy in copies:
                copy.wait_recv()
            flag_a = [s >= 1, s >= 2]
            flag_b = [m >= 1, (m >= 1) & (s >= 1), (m >= 1) & (s >= 2)]
            for c in range(2):
                terms = []
                for p in range(3):
                    term = sums[it, p, c, 0:tile, :]
                    for i in range(2):
                        term = term + jnp.where(flag_a[i], land_a[it, i, p, c], 0.0)
                    if c == 0:
                        for i in range(3):
                            term = term + jnp.where(flag_b[i], land_b[it, i, p], 0.0)
                    terms.append(term)
                for p in range(2):
                    fresh = ext[it, p, c, 0:tile, :] + terms[p] / (terms[2] + 1.0)
                    if it == ITERS - 1:
                        obj_out[p, :, c * N : (c + 1) * N] = fresh
                    else:
                        ext[it + 1, p, c, 0:tile, :] = fresh

        for it in range(ITERS):
            for copy in halo_copies:
                copy.wait_recv()
            for j in range(2):
                position(it, j)
            steps = reduce_steps(it)
            next(steps)
            next(steps)
            sum_copies = start_sums(it)
            next(steps)
            next(steps)
            finish_sums(it, sum_copies)
            if it + 1 < ITERS:
                halo_copies = start_halo(it + 1)
            for _ in steps:
                pass
        probe_out[0] = probes[ITERS, own_mode]
        for copy in started:
            copy.wait_send()

    return kernel


def scratch_of(plan):
    n_mode, side, tile = plan.n_mode, plan.side, plan.tile
    planes, half, rows, own = plan.planes, plan.half, plan.rows, plan.own_planes
    rows_all = n_mode * N

    def vmem(*shape, kind=F32):
        return pltpu.VMEM(shape, kind)

    def sems(*shape):
        return [pltpu.SemaphoreType.DMA(shape), pltpu.SemaphoreType.DMA(shape)]

    return [
        vmem(ITERS, 2, 3, 3 * tile, N),
        vmem(ITERS + 1, planes, N, N),
        vmem(ITERS, 3, 3, 3 * tile, N),
        vmem(3, 4, 256, N),
        vmem(2, N, N),
        vmem(rows_all, 2 * N),
        vmem(rows_all, 2 * N, kind=BF16),
        vmem(rows_all, 2 * N, kind=BF16),
        vmem(2 * N, rows_all, kind=BF16),
        vmem(2 * N, rows_all, kind=BF16),
        vmem(ITERS, planes + 1, N, N),
        vmem(ITERS, planes + 1, half, N),
        vmem(ITERS, planes + 1, half, N),
        vmem(ITERS, side - 1, planes + 1, rows, N),
        vmem(ITERS, side, own + 1, rows, N),
        vmem(ITERS, side - 1, own + 1, rows, N),
        vmem(ITERS, n_mode, own + 1, rows, N),
        vmem(8, N),
        vmem(ITERS, 2, 3, 2, tile, N),
        vmem(ITERS, 3, 3, tile, N),
        *sems(n_mode - 1),
        *sems(n_mode - 1),
        *sems(ITERS, 5),
        *sems(ITERS, 5),
        *sems(ITERS),
        *sems(ITERS, side - 1),
        *sems(ITERS, side - 1),
        *sems(ITERS, n_mode - 1),
        *sems(ITERS, side - 1),
        *sems(ITERS, side - 1),
        *sems(ITERS),
    ]


def solution(mesh):
    n_scan, n_mode = mesh.shape["scan"], mesh.shape["mode"]
    left_np, right_np = fresnel_blocks()

    def local(object_field, probe, amplitude, offsets, counts):
        plan = Plan(n_scan, n_mode, object_field.shape[1])
        in_vmem = pl.BlockSpec(memory_space=pltpu.VMEM)
        in_smem = pl.BlockSpec(memory_space=pltpu.SMEM)
        return pl.pallas_call(
            make_kernel(plan),
            out_shape=(
                jax.ShapeDtypeStruct(object_field.shape, F32),
                jax.ShapeDtypeStruct(probe.shape, F32),
            ),
            in_specs=[in_vmem] * 5 + [in_smem] * 2,
            out_specs=(in_vmem, in_vmem),
            scratch_shapes=scratch_of(plan),
            compiler_params=pltpu.CompilerParams(
                collective_id=0, has_side_effects=True, vmem_limit_bytes=40 * 1024 * 1024
            ),
        )(object_field, probe, amplitude, jnp.asarray(left_np), jnp.asarray(right_np), offsets, counts)

    placed = (
        P(None, "scan", "mode"),
        P("mode", None, None, None),
        P(("scan", "mode"), None, None),
        P(("scan", "mode"), None),
        P(("scan", "mode")),
    )
    return jax.shard_map(
        local,
        mesh=mesh,
        in_specs=placed,
        out_specs=(P(None, "scan", "mode"), P("mode", None, None, None)),
        check_vma=False,
    )
```

```python
import math

import jax
import jax.numpy as jnp
import ml_dtypes
import numpy as np
from jax import lax
from jax.experimental import pallas as pl
from jax.experimental.pallas import tpu as pltpu
from jax.sharding import PartitionSpec as P

ITERS = 2
CORES = 2
N = 128
SPLIT_RINGS = (True, True)
MESH = pl.DeviceIdType.MESH
F32 = jnp.float32
BF16 = jnp.bfloat16


def fresnel_blocks():
    ids = np.arange(N)
    phase = (ids[:, None] * ids[None, :]) % N
    chirp = ((ids - N // 2) ** 2) % (4 * N)
    angle = -2.0 * math.pi / N * phase + math.pi / (2 * N) * chirp[None, :]
    re, im = np.cos(angle) / math.sqrt(N), np.sin(angle) / math.sqrt(N)
    full = np.block([[re, -im], [im, re]]).astype(np.float32)

    def parts(matrix):
        high = matrix.astype(ml_dtypes.bfloat16)
        low = (matrix - high.astype(np.float32)).astype(ml_dtypes.bfloat16)
        return np.stack([high, low])

    return parts(full), parts(np.ascontiguousarray(full.T))


def split(value):
    high = value.astype(BF16)
    return high, (value - high.astype(F32)).astype(BF16)


def dot(first, second):
    return jnp.dot(first, second, preferred_element_type=F32)


def dot3(first_high, first_low, second_high, second_low):
    return dot(first_high, second_high) + dot(first_high, second_low) + dot(first_low, second_high)


class Plan:
    def __init__(self, n_scan, n_mode, tile_rows):
        self.n_scan, self.n_mode, self.tile = n_scan, n_mode, tile_rows
        self.side = math.isqrt(n_scan // CORES)
        assert self.side * self.side * CORES == n_scan
        self.planes = 2 * n_mode
        self.half = N // CORES
        self.rows = self.half // self.side


def make_kernel(plan):
    n_scan, n_mode, tile, side = plan.n_scan, plan.n_mode, plan.tile, plan.side
    planes, half, rows = plan.planes, plan.half, plan.rows
    far_rows = n_scan * tile
    far_cols = n_mode * 2 * N

    def kernel(
        obj_hbm, probe_hbm, amp_hbm, left_hbm, right_hbm, off_ref, cnt_ref,
        obj_out, probe_out,
        ext, probes, amp_ref, left_ref, right_ref, sums, pad, patch, exits, ah, al, xh, xl,
        grad, land_core, acc_core, land_x, acc_x, land_ring, all_b,
        land_down, folded, land_beside,
        s_in, s_probe, r_probe, s_fwd, r_fwd, s_halo, r_halo, s_down, r_down, s_beside, r_beside,
        s_core, r_core, s_x, r_x, s_ring, r_ring, s_all, r_all,
        s_gather, r_gather, s_modes, r_modes, s_back, r_back,
    ):
        s = lax.axis_index("scan")
        m = lax.axis_index("mode")
        core = lax.rem(s, CORES)
        chip = lax.div(s, CORES)
        y, z = lax.rem(chip, side), lax.div(chip, side)
        other = (s + 1 - 2 * core, m)

        def near(ds, dm):
            return (lax.rem(s + ds + n_scan, n_scan), lax.rem(m + dm + n_mode, n_mode))

        ring_y = [((z * side + lax.rem(y + d, side)) * CORES + core, m) for d in range(1, side)]
        ring_z = [((lax.rem(z + d, side) * side + y) * CORES + core, m) for d in range(1, side)]
        peers_x = [near(0, d) for d in range(1, n_mode)]
        halo_steps = [(1, 0), (2, 0), (0, 1), (1, 1), (2, 1)]
        before = [near(-ds, -dm) for ds, dm in halo_steps]
        after = [near(ds, dm) for ds, dm in halo_steps]
        peers = [other] + ring_y + ring_z + peers_x + before + after

        started = []

        def send(src, dst, send_sem, recv_sem, device):
            copy = pltpu.make_async_remote_copy(
                src_ref=src, dst_ref=dst, send_sem=send_sem, recv_sem=recv_sem,
                device_id=device, device_id_type=MESH,
            )
            copy.start()
            started.append(copy)
            return copy

        barrier = pltpu.get_barrier_semaphore()
        for device in peers:
            pl.semaphore_signal(barrier, inc=1, device_id=device, device_id_type=MESH)

        fetched = [
            pltpu.make_async_copy(obj_hbm.at[:, :, pl.ds(0, N)], ext.at[0, :, 0, pl.ds(0, tile), :], s_in.at[0]),
            pltpu.make_async_copy(obj_hbm.at[:, :, pl.ds(N, N)], ext.at[0, :, 1, pl.ds(0, tile), :], s_in.at[1]),
            pltpu.make_async_copy(probe_hbm.at[0], probes.at[0, pl.ds(2 * m, 2)], s_in.at[2]),
            pltpu.make_async_copy(right_hbm, right_ref, s_in.at[3]),
            pltpu.make_async_copy(left_hbm, left_ref, s_in.at[4]),
            pltpu.make_async_copy(amp_hbm, amp_ref, s_in.at[5]),
        ]
        for copy in fetched:
            copy.start()
        zero_half = jnp.zeros((64, N), F32)
        zero_block = jnp.zeros((256, N), F32)
        for p in range(3):
            pad[p, 0] = zero_block
            pad[p, 3] = zero_block
            for c in (1, 2):
                pad[p, c, 0:64, :] = zero_half
                pad[p, c, 192:256, :] = zero_half

        for copy in fetched[:3]:
            copy.wait()
        pl.semaphore_wait(barrier, len(peers))

        def start_halo(it):
            copies = []
            for i in (1, 2):
                copies.append(
                    send(ext.at[it, :, pl.ds(0, 2), pl.ds(0, tile), :],
                         ext.at[it, :, pl.ds(0, 2), pl.ds(i * tile, tile), :],
                         s_halo.at[it, i - 1], r_halo.at[it, i - 1], before[i - 1])
                )
            for i in range(3):
                copies.append(
                    send(ext.at[it, :, 0, pl.ds(0, tile), :],
                         ext.at[it, :, 2, pl.ds(i * tile, tile), :],
                         s_halo.at[it, 2 + i], r_halo.at[it, 2 + i], before[2 + i])
                )
            return copies

        mine = pl.ds(core * half, half)
        own_mode = pl.ds(2 * m, 2)
        probe_copies = [
            send(probes.at[0, own_mode, mine, :], probes.at[0, own_mode, mine, :],
                 s_probe.at[d - 1], r_probe.at[d - 1], peers_x[d - 1])
            for d in range(1, n_mode)
        ]
        halo_copies = start_halo(0)
        forwards = []
        for d in range(1, n_mode):
            probe_copies[d - 1].wait_recv()
            came = pl.ds(2 * lax.rem(m - d + n_mode, n_mode), 2)
            forwards.append(
                send(probes.at[0, came, mine, :], probes.at[0, came, mine, :],
                     s_fwd.at[d - 1], r_fwd.at[d - 1], other)
            )
        for copy in forwards:
            copy.wait_recv()

        for copy in fetched[3:]:
            copy.wait()

        lane = lax.broadcasted_iota(jnp.int32, (N, N), 1)
        row_id = lax.broadcasted_iota(jnp.int32, (N, N), 0)

        def position(it, j):
            top, leftmost = off_ref[j, 0], off_ref[j, 1]
            row, col = lax.rem(top, tile), lax.rem(leftmost, 2 * N)
            col_block, col_lane = lax.div(col, N), lax.rem(col, N)
            used = jnp.where(j < cnt_ref[0], 1.0, 0.0).astype(F32)
            back_shift = lax.rem(N - col_lane, N)
            inside = (row_id + top < far_rows) & (lane + leftmost < far_cols)
            for p in range(2):
                one = ext[it, p, col_block, pl.ds(row, N), :]
                two = ext[it, p, col_block + 1, pl.ds(row, N), :]
                moved = pltpu.roll(jnp.where(lane >= col_lane, one, two), back_shift, 1)
                patch[p] = jnp.where(inside, moved, 0.0)
            for k in range(n_mode):
                spot = pl.ds(k * N, N)
                pr, pi = probes[it, 2 * k], probes[it, 2 * k + 1]
                o_re, o_im = patch[0], patch[1]
                e_re = pr * o_re - pi * o_im
                e_im = pr * o_im + pi * o_re
                for c, value in ((0, e_re), (1, e_im)):
                    where_c = pl.ds(c * N, N)
                    exits[spot, where_c] = value
                    high, low = split(value)
                    ah[spot, where_c] = high
                    al[spot, where_c] = low
            mid = dot3(ah[...], al[...], right_ref[0], right_ref[1])
            high, low = split(mid)
            for k in range(n_mode):
                for c in range(2):
                    block = (slice(k * N, (k + 1) * N), slice(c * N, (c + 1) * N))
                    turned = (pl.ds(c * N, N), pl.ds(k * N, N))
                    xh[turned] = high[block]
                    xl[turned] = low[block]
            far = dot3(left_ref[0], left_ref[1], xh[...], xl[...])
            intensity = jnp.zeros((N, N), F32)
            for k in range(n_mode):
                for c in range(2):
                    part = far[c * N : (c + 1) * N, k * N : (k + 1) * N]
                    intensity = intensity + part * part
            factor = amp_ref[j] / jnp.sqrt(jnp.maximum(intensity, 1.0))
            for k in range(n_mode):
                for c in range(2):
                    part = far[c * N : (c + 1) * N, k * N : (k + 1) * N] * factor
                    high, low = split(part)
                    xh[pl.ds(c * N, N), pl.ds(k * N, N)] = high
                    xl[pl.ds(c * N, N), pl.ds(k * N, N)] = low
            back = dot3(right_ref[0], right_ref[1], xh[...], xl[...])
            high, low = split(back)
            for k in range(n_mode):
                for c in range(2):
                    block = (slice(c * N, (c + 1) * N), slice(k * N, (k + 1) * N))
                    turned = (pl.ds(k * N, N), pl.ds(c * N, N))
                    ah[turned] = high[block]
                    al[turned] = low[block]
            near_field = dot3(ah[...], al[...], left_ref[0], left_ref[1])
            exits[...] = near_field - exits[...]
            num_re = jnp.zeros((N, N), F32)
            num_im = jnp.zeros((N, N), F32)
            weight = jnp.zeros((N, N), F32)
            o_re, o_im = patch[0] * used, patch[1] * used
            for k in range(n_mode):
                spot = pl.ds(k * N, N)
                c_re, c_im = exits[spot, pl.ds(0, N)], exits[spot, pl.ds(N, N)]
                pr, pi = probes[it, 2 * k], probes[it, 2 * k + 1]
                num_re = num_re + (pr * c_re + pi * c_im)
                num_im = num_im + (pr * c_im - pi * c_re)
                weight = weight + (pr * pr + pi * pi)
                g_re = o_re * c_re + o_im * c_im
                g_im = o_re * c_im - o_im * c_re
                if j == 0:
                    grad[it, 2 * k] = g_re
                    grad[it, 2 * k + 1] = g_im
                else:
                    grad[it, 2 * k] += g_re
                    grad[it, 2 * k + 1] += g_im
            density = o_re * patch[0] + o_im * patch[1]
            if j == 0:
                grad[it, planes] = density
            else:
                grad[it, planes] += density
            for p, value in enumerate((num_re, num_im, weight)):
                moved = pltpu.roll(value * used, col_lane, 1)
                pad[p, 1, 64:192, :] = jnp.where(lane >= col_lane, moved, 0.0)
                pad[p, 2, 64:192, :] = jnp.where(lane < col_lane, moved, 0.0)
            for p in range(3):
                for c in range(3):
                    placed = pad[p, c + 1 - col_block, pl.ds(64 - row, 192), :]
                    if j == 0:
                        sums[it, p, c] = placed
                    else:
                        sums[it, p, c] += placed

        def reduce_steps(it):
            last = it == ITERS - 1
            split_rings = SPLIT_RINGS[it]
            a = z * (1 - core) + y * core if split_rings else z
            b = y * (1 - core) + z * core if split_rings else y

            def at(first, second):
                if split_rings:
                    yy = second * (1 - core) + first * core
                    zz = first * (1 - core) + second * core
                else:
                    yy, zz = second, first
                return ((zz * side + yy) * CORES + core, m)

            peers_a = [(lax.rem(a + d, side), at(lax.rem(a + d, side), b)) for d in range(1, side)]
            peers_b = [at(a, lax.rem(b + d, side)) for d in range(1, side)]
            theirs = pl.ds((1 - core) * half, half)
            copy = send(grad.at[it, :, theirs, :], land_core.at[it], s_core.at[it], r_core.at[it], other)
            yield
            copy.wait_recv()
            density = grad[it, planes, mine, :] + land_core[it, planes]
            for k in range(n_mode):
                for c in range(2):
                    acc_core[it, k, c] = grad[it, 2 * k + c, mine, :] + land_core[it, 2 * k + c]
                acc_core[it, k, 2] = density
            copies = [
                send(acc_core.at[it, lax.rem(m + d, n_mode)], land_x.at[it, d - 1],
                     s_x.at[it, d - 1], r_x.at[it, d - 1], peers_x[d - 1])
                for d in range(1, n_mode)
            ]
            yield
            for copy in copies:
                copy.wait_recv()
            for c in range(3):
                total = acc_core[it, m, c]
                for d in range(1, n_mode):
                    total = total + land_x[it, d - 1, c]
                acc_x[it, c] = total
            copies = [
                send(acc_x.at[it, :, pl.ds(pl.multiple_of(t * rows, rows), rows), :], land_ring.at[it, i],
                     s_ring.at[it, i], r_ring.at[it, i], device)
                for i, (t, device) in enumerate(peers_a)
            ]
            yield
            total = acc_x[it, :, pl.ds(pl.multiple_of(a * rows, rows), rows), :]
            for i, copy in enumerate(copies):
                copy.wait_recv()
                total = total + land_ring[it, i]
            all_b[it, b] = total
            copies = [
                send(all_b.at[it, b], all_b.at[it, b], s_all.at[it, i], r_all.at[it, i], device)
                for i, device in enumerate(peers_b)
            ]
            yield
            for copy in copies:
                copy.wait_recv()
            total = all_b[it, 0]
            for i in range(1, side):
                total = total + all_b[it, i]
            spot = pl.ds(pl.multiple_of(core * half + a * rows, rows), rows)
            probes[it + 1, own_mode, spot, :] = probes[it, own_mode, spot, :] + total[0:2] / (total[2:3] + 1.0)
            piece = probes.at[it + 1, own_mode, spot, :]
            copies = [
                send(piece, piece, s_gather.at[it, i], r_gather.at[it, i], device)
                for i, (t, device) in enumerate(peers_a)
            ]
            yield
            for copy in copies:
                copy.wait_recv()
            piece = probes.at[it + 1, own_mode, mine, :]
            backs = [send(piece, piece, s_back.at[it, 0], r_back.at[it, 0], other)]
            if not last:
                copies = [
                    send(piece, piece, s_modes.at[it, d - 1], r_modes.at[it, d - 1], peers_x[d - 1])
                    for d in range(1, n_mode)
                ]
                yield
                for d in range(1, n_mode):
                    copies[d - 1].wait_recv()
                    came = pl.ds(2 * lax.rem(m - d + n_mode, n_mode), 2)
                    piece = probes.at[it + 1, came, mine, :]
                    backs.append(send(piece, piece, s_back.at[it, d], r_back.at[it, d], other))
            yield
            for copy in backs:
                copy.wait_recv()

        def terms_down(it):
            return [
                send(sums.at[it, :, :, pl.ds(i * tile, tile), :], land_down.at[it, i - 1],
                     s_down.at[it, i - 1], r_down.at[it, i - 1], after[i - 1])
                for i in (1, 2)
            ]

        def terms_beside(it, copies):
            for copy in copies:
                copy.wait_recv()
            for p in range(3):
                for c in range(3):
                    term = sums[it, p, c, 0:tile, :]
                    for i in range(2):
                        term = term + jnp.where(s > i, land_down[it, i, p, c], 0.0)
                    folded[it, c, p] = term
            return send(folded.at[it, 2], land_beside.at[it], s_beside.at[it], r_beside.at[it], after[2])

        def new_object(it, copy):
            copy.wait_recv()
            for c in range(2):
                terms = []
                for p in range(3):
                    term = folded[it, c, p]
                    if c == 0:
                        term = term + jnp.where(m > 0, land_beside[it, p], 0.0)
                    terms.append(term)
                for p in range(2):
                    fresh = ext[it, p, c, 0:tile, :] + terms[p] / (terms[2] + 1.0)
                    if it == ITERS - 1:
                        obj_out[p, :, c * N : (c + 1) * N] = fresh
                    else:
                        ext[it + 1, p, c, 0:tile, :] = fresh

        for it in range(ITERS):
            for copy in halo_copies:
                copy.wait_recv()
            for j in range(2):
                position(it, j)
            steps = reduce_steps(it)
            next(steps)
            down = terms_down(it)
            next(steps)
            next(steps)
            beside = terms_beside(it, down)
            next(steps)
            new_object(it, beside)
            if it + 1 < ITERS:
                halo_copies = start_halo(it + 1)
            for _ in steps:
                pass
        probe_out[0] = probes[ITERS, own_mode]
        for copy in started:
            copy.wait_send()

    return kernel


def scratch_of(plan):
    n_mode, side, tile = plan.n_mode, plan.side, plan.tile
    planes, half, rows = plan.planes, plan.half, plan.rows
    rows_all = n_mode * N

    def vmem(*shape, kind=F32):
        return pltpu.VMEM(shape, kind)

    def sems(*shape):
        return [pltpu.SemaphoreType.DMA(shape), pltpu.SemaphoreType.DMA(shape)]

    return [
        vmem(ITERS, 2, 3, 3 * tile, N),
        vmem(ITERS + 1, planes, N, N),
        vmem(2, N, N),
        vmem(2, 2 * N, 2 * N, kind=BF16),
        vmem(2, 2 * N, 2 * N, kind=BF16),
        vmem(ITERS, 3, 3, 3 * tile, N),
        vmem(3, 4, 256, N),
        vmem(2, N, N),
        vmem(rows_all, 2 * N),
        vmem(rows_all, 2 * N, kind=BF16),
        vmem(rows_all, 2 * N, kind=BF16),
        vmem(2 * N, rows_all, kind=BF16),
        vmem(2 * N, rows_all, kind=BF16),
        vmem(ITERS, planes + 1, N, N),
        vmem(ITERS, planes + 1, half, N),
        vmem(ITERS, n_mode, 3, half, N),
        vmem(ITERS, n_mode - 1, 3, half, N),
        vmem(ITERS, 3, half, N),
        vmem(ITERS, side - 1, 3, rows, N),
        vmem(ITERS, side, 3, rows, N),
        vmem(ITERS, 2, 3, 3, tile, N),
        vmem(ITERS, 3, 3, tile, N),
        vmem(ITERS, 3, tile, N),
        pltpu.SemaphoreType.DMA((6,)),
        *sems(n_mode - 1),
        *sems(n_mode - 1),
        *sems(ITERS, 5),
        *sems(ITERS, 2),
        *sems(ITERS),
        *sems(ITERS),
        *sems(ITERS, n_mode - 1),
        *sems(ITERS, side - 1),
        *sems(ITERS, side - 1),
        *sems(ITERS, side - 1),
        *sems(ITERS, n_mode - 1),
        *sems(ITERS, n_mode),
    ]


def solution(mesh):
    n_scan, n_mode = mesh.shape["scan"], mesh.shape["mode"]
    left_np, right_np = fresnel_blocks()

    def local(object_field, probe, amplitude, offsets, counts):
        plan = Plan(n_scan, n_mode, object_field.shape[1])
        in_vmem = pl.BlockSpec(memory_space=pltpu.VMEM)
        in_smem = pl.BlockSpec(memory_space=pltpu.SMEM)
        return pl.pallas_call(
            make_kernel(plan),
            out_shape=(
                jax.ShapeDtypeStruct(object_field.shape, F32),
                jax.ShapeDtypeStruct(probe.shape, F32),
            ),
            in_specs=[pl.BlockSpec(memory_space=pltpu.HBM)] * 5 + [in_smem] * 2,
            out_specs=(in_vmem, in_vmem),
            scratch_shapes=scratch_of(plan),
            compiler_params=pltpu.CompilerParams(
                collective_id=0, has_side_effects=True, vmem_limit_bytes=60 * 1024 * 1024
            ),
        )(object_field, probe, amplitude, jnp.asarray(left_np), jnp.asarray(right_np), offsets, counts)

    placed = (
        P(None, "scan", "mode"),
        P("mode", None, None, None),
        P(("scan", "mode"), None, None),
        P(("scan", "mode"), None),
        P(("scan", "mode")),
    )
    return jax.shard_map(
        local,
        mesh=mesh,
        in_specs=placed,
        out_specs=(P(None, "scan", "mode"), P("mode", None, None, None)),
        check_vma=False,
    )
```

```python
import math

import jax
import jax.numpy as jnp
import ml_dtypes
import numpy as np
from jax import lax
from jax.experimental import pallas as pl
from jax.experimental.pallas import tpu as pltpu
from jax.sharding import PartitionSpec as P

ITERS = 2
CORES = 2
N = 128
SPLIT_RINGS = (True, True)
MESH = pl.DeviceIdType.MESH
F32 = jnp.float32
BF16 = jnp.bfloat16


def fresnel_blocks():
    ids = np.arange(N)
    phase = (ids[:, None] * ids[None, :]) % N
    chirp = ((ids - N // 2) ** 2) % (4 * N)
    angle = -2.0 * math.pi / N * phase + math.pi / (2 * N) * chirp[None, :]
    re, im = np.cos(angle) / math.sqrt(N), np.sin(angle) / math.sqrt(N)
    full = np.block([[re, -im], [im, re]]).astype(np.float32)

    def parts(matrix):
        high = matrix.astype(ml_dtypes.bfloat16)
        low = (matrix - high.astype(np.float32)).astype(ml_dtypes.bfloat16)
        return np.stack([high, low])

    return parts(full), parts(np.ascontiguousarray(full.T))


def split(value):
    high = value.astype(BF16)
    return high, (value - high.astype(F32)).astype(BF16)


def dot(first, second):
    return jnp.dot(first, second, preferred_element_type=F32)


def dot3(first_high, first_low, second_high, second_low):
    return dot(first_high, second_high) + dot(first_high, second_low) + dot(first_low, second_high)


class Plan:
    def __init__(self, n_scan, n_mode, tile_rows):
        self.n_scan, self.n_mode, self.tile = n_scan, n_mode, tile_rows
        self.side = math.isqrt(n_scan // CORES)
        assert self.side * self.side * CORES == n_scan
        self.planes = 2 * n_mode
        self.half = N // CORES
        self.rows = self.half // self.side


def make_kernel(plan):
    n_scan, n_mode, tile, side = plan.n_scan, plan.n_mode, plan.tile, plan.side
    planes, half, rows = plan.planes, plan.half, plan.rows
    far_rows = n_scan * tile
    far_cols = n_mode * 2 * N

    def kernel(
        obj_hbm, probe_hbm, amp_hbm, left_hbm, right_hbm, off_ref, cnt_ref,
        obj_out, probe_out,
        ext, probes, amp_ref, left_ref, right_ref, sums, pad, patch, exits, ah, al, xh, xl, far, factor, num,
        grad, land_core, acc_core, land_x, acc_x, land_ring, all_b,
        land_weight, land_edge, land_down, folded, land_beside,
        s_in, s_probe, r_probe, s_fwd, r_fwd, s_halo, r_halo, s_weight, r_weight, s_down, r_down, s_beside, r_beside,
        s_core, r_core, s_x, r_x, s_ring, r_ring, s_all, r_all,
        s_gather, r_gather,
    ):
        s = lax.axis_index("scan")
        m = lax.axis_index("mode")
        core = lax.rem(s, CORES)
        chip = lax.div(s, CORES)
        y, z = lax.rem(chip, side), lax.div(chip, side)
        other = (s + 1 - 2 * core, m)

        def near(ds, dm):
            return (lax.rem(s + ds + n_scan, n_scan), lax.rem(m + dm + n_mode, n_mode))

        ring_y = [((z * side + lax.rem(y + d, side)) * CORES + core, m) for d in range(1, side)]
        ring_z = [((lax.rem(z + d, side) * side + y) * CORES + core, m) for d in range(1, side)]
        peers_x = [near(0, d) for d in range(1, n_mode)]
        halo_steps = [(1, 0), (2, 0), (0, 1), (1, 1), (2, 1)]
        before = [near(-ds, -dm) for ds, dm in halo_steps]
        after = [near(ds, dm) for ds, dm in halo_steps]
        peers = [other] + ring_y + ring_z + peers_x + before + after

        started = []

        def send(src, dst, send_sem, recv_sem, device):
            copy = pltpu.make_async_remote_copy(
                src_ref=src, dst_ref=dst, send_sem=send_sem, recv_sem=recv_sem,
                device_id=device, device_id_type=MESH,
            )
            copy.start()
            started.append(copy)
            return copy

        barrier = pltpu.get_barrier_semaphore()
        for device in peers:
            pl.semaphore_signal(barrier, inc=1, device_id=device, device_id_type=MESH)

        fetched = [
            pltpu.make_async_copy(obj_hbm.at[:, :, pl.ds(0, N)], ext.at[0, :, 0, pl.ds(0, tile), :], s_in.at[0]),
            pltpu.make_async_copy(obj_hbm.at[:, :, pl.ds(N, N)], ext.at[0, :, 1, pl.ds(0, tile), :], s_in.at[1]),
            pltpu.make_async_copy(probe_hbm.at[0], probes.at[0, pl.ds(2 * m, 2)], s_in.at[2]),
            pltpu.make_async_copy(right_hbm, right_ref, s_in.at[3]),
            pltpu.make_async_copy(left_hbm, left_ref, s_in.at[4]),
            pltpu.make_async_copy(amp_hbm, amp_ref, s_in.at[5]),
        ]
        for copy in fetched:
            copy.start()
        zero_half = jnp.zeros((64, N), F32)
        zero_block = jnp.zeros((256, N), F32)
        for j in range(2):
            for p in range(3):
                pad[j, p, 0] = zero_block
                pad[j, p, 3] = zero_block
                for c in (1, 2):
                    pad[j, p, c, 0:64, :] = zero_half
                    pad[j, p, c, 192:256, :] = zero_half

        for copy in fetched[:3]:
            copy.wait()
        pl.semaphore_wait(barrier, len(peers))

        def start_halo(it):
            copies = []
            for i in (1, 2):
                copies.append(
                    send(ext.at[it, :, pl.ds(0, 2), pl.ds(0, tile), :],
                         ext.at[it, :, pl.ds(0, 2), pl.ds(i * tile, tile), :],
                         s_halo.at[it, i - 1], r_halo.at[it, i - 1], before[i - 1])
                )
            for i in range(3):
                copies.append(
                    send(ext.at[it, :, 0, pl.ds(0, tile), :],
                         ext.at[it, :, 2, pl.ds(i * tile, tile), :],
                         s_halo.at[it, 2 + i], r_halo.at[it, 2 + i], before[2 + i])
                )
            return copies

        mine = pl.ds(core * half, half)
        theirs = pl.ds((1 - core) * half, half)
        own_mode = pl.ds(2 * m, 2)
        arrival = [d for d in range(1, n_mode) if d != n_mode // 2] + [n_mode // 2]

        pairs = side // 2
        wide = 2 * rows

        def flipped(value, mask):
            out, bit = value, 1
            while bit <= mask:
                if mask & bit:
                    out = out + bit - 2 * bit * lax.rem(lax.div(value, bit), 2)
                bit *= 2
            return out

        far_first = sorted(range(pairs), key=lambda e: (e != pairs // 2, e == 0, e))

        def ring_of(it):
            return y * core + z * (1 - core) if SPLIT_RINGS[it] else z

        def block_of(it):
            return lax.div(ring_of(it), 2)

        def mode_of(d):
            return lax.rem(m - d + n_mode, n_mode)

        def send_mode(it, e, where):
            piece = probes.at[it, own_mode, where, :]
            return {d: send(piece, piece, s_probe.at[it, d, e], r_probe.at[it, d, e], near(0, d)) for d in arrival}

        def trade(it, d):
            piece = probes.at[it, pl.ds(2 * mode_of(d), 2), mine, :]
            return send(piece, piece, s_fwd.at[it, d], r_fwd.at[it, d], other)

        probe_copies = [send_mode(0, 0, mine)]
        halo_copies = start_halo(0)
        trades = {}

        lane = lax.broadcasted_iota(jnp.int32, (N, N), 1)
        row_id = lax.broadcasted_iota(jnp.int32, (N, N), 0)

        def used_of(j):
            return jnp.where(j < cnt_ref[0], 1.0, 0.0).astype(F32)

        def spot_of(j):
            row, col = lax.rem(off_ref[j, 0], tile), lax.rem(off_ref[j, 1], 2 * N)
            return row, lax.div(col, N), lax.rem(col, N)

        def take_patches(it):
            density = jnp.zeros((N, N), F32)
            for j in range(2):
                row, col_block, col_lane = spot_of(j)
                inside = (row_id + off_ref[j, 0] < far_rows) & (lane + off_ref[j, 1] < far_cols)
                for p in range(2):
                    one = ext[it, p, col_block, pl.ds(row, N), :]
                    two = ext[it, p, col_block + 1, pl.ds(row, N), :]
                    moved = pltpu.roll(jnp.where(lane >= col_lane, one, two), lax.rem(N - col_lane, N), 1)
                    moved = jnp.where(inside, moved, 0.0)
                    patch[j, p] = moved
                    density = density + moved * moved * used_of(j)
            grad[it, planes] = density

        def forward(it, d):
            k = mode_of(d)
            pr, pi = probes[it, 2 * k], probes[it, 2 * k + 1]
            for j in range(2):
                rows_j = pl.ds(j * N, N)
                o_re, o_im = patch[j, 0], patch[j, 1]
                for c, value in ((0, pr * o_re - pi * o_im), (1, pr * o_im + pi * o_re)):
                    cols_c = pl.ds(c * N, N)
                    exits[d, rows_j, cols_c] = value
                    high, low = split(value)
                    ah[d, rows_j, cols_c] = high
                    al[d, rows_j, cols_c] = low
            high, low = split(dot3(ah[d], al[d], right_ref[0], right_ref[1]))
            for j in range(2):
                for c in range(2):
                    block = (slice(j * N, (j + 1) * N), slice(c * N, (c + 1) * N))
                    xh[d, pl.ds(c * N, N), pl.ds(j * N, N)] = high[block]
                    xl[d, pl.ds(c * N, N), pl.ds(j * N, N)] = low[block]
            far[d] = dot3(left_ref[0], left_ref[1], xh[d], xl[d])

        def set_factors():
            for j in range(2):
                intensity = jnp.zeros((N, N), F32)
                for d in range(n_mode):
                    for c in range(2):
                        part = far[d, pl.ds(c * N, N), pl.ds(j * N, N)]
                        intensity = intensity + part * part
                factor[j] = amp_ref[j] / jnp.sqrt(jnp.maximum(intensity, 1.0))

        def backward(it, d, first):
            k = mode_of(d)
            for j in range(2):
                for c in range(2):
                    block = (pl.ds(c * N, N), pl.ds(j * N, N))
                    high, low = split(far[(d,) + block] * factor[j])
                    xh[(d,) + block] = high
                    xl[(d,) + block] = low
            high, low = split(dot3(right_ref[0], right_ref[1], xh[d], xl[d]))
            for j in range(2):
                for c in range(2):
                    block = (slice(c * N, (c + 1) * N), slice(j * N, (j + 1) * N))
                    ah[d, pl.ds(j * N, N), pl.ds(c * N, N)] = high[block]
                    al[d, pl.ds(j * N, N), pl.ds(c * N, N)] = low[block]
            change = dot3(ah[d], al[d], left_ref[0], left_ref[1]) - exits[d]
            pr, pi = probes[it, 2 * k], probes[it, 2 * k + 1]
            g_re = jnp.zeros((N, N), F32)
            g_im = jnp.zeros((N, N), F32)
            for j in range(2):
                c_re = change[j * N : (j + 1) * N, 0:N]
                c_im = change[j * N : (j + 1) * N, N : 2 * N]
                o_re, o_im = patch[j, 0] * used_of(j), patch[j, 1] * used_of(j)
                g_re = g_re + (o_re * c_re + o_im * c_im)
                g_im = g_im + (o_re * c_im - o_im * c_re)
                n_re = pr * c_re + pi * c_im
                n_im = pr * c_im - pi * c_re
                if first:
                    num[j, 0] = n_re
                    num[j, 1] = n_im
                else:
                    num[j, 0] += n_re
                    num[j, 1] += n_im
            grad[it, 2 * k] = g_re
            grad[it, 2 * k + 1] = g_im

        def set_pad(j, p, value):
            _, _, col_lane = spot_of(j)
            moved = pltpu.roll(value * used_of(j), col_lane, 1)
            pad[j, p, 1, 64:192, :] = jnp.where(lane >= col_lane, moved, 0.0)
            pad[j, p, 2, 64:192, :] = jnp.where(lane < col_lane, moved, 0.0)

        def placed(p, c):
            row_0, block_0, _ = spot_of(0)
            row_1, block_1, _ = spot_of(1)
            return (
                pad[0, p, c + 1 - block_0, pl.ds(64 - row_0, 192), :]
                + pad[1, p, c + 1 - block_1, pl.ds(64 - row_1, 192), :]
            )

        def weight_down(it):
            weight = jnp.zeros((N, N), F32)
            for p in range(planes):
                weight = weight + probes[it, p] * probes[it, p]
            for j in range(2):
                set_pad(j, 2, weight)
            for c in range(3):
                sums[it, c, 2] = placed(2, c)
            return [
                send(sums.at[it, :, 2, pl.ds(i * tile, tile), :], land_weight.at[it, i - 1],
                     s_weight.at[it, i - 1], r_weight.at[it, i - 1], after[i - 1])
                for i in (1, 2)
            ]

        def terms_down(it):
            for j in range(2):
                for p in range(2):
                    set_pad(j, p, num[j, p])
            copies = []
            for p in range(2):
                sums[it, 2, p] = placed(p, 2)
            for i in (1, 2):
                copies.append(
                    send(sums.at[it, 2, pl.ds(0, 2), pl.ds(i * tile, tile), :], land_edge.at[it, i - 1],
                         s_down.at[it, i - 1], r_down.at[it, i - 1], after[i - 1])
                )
            for c in range(2):
                for p in range(2):
                    sums[it, c, p] = placed(p, c)
            for i in (1, 2):
                copies.append(
                    send(sums.at[it, pl.ds(0, 2), pl.ds(0, 2), pl.ds(i * tile, tile), :], land_down.at[it, i - 1],
                         s_down.at[it, i + 1], r_down.at[it, i + 1], after[i - 1])
                )
            return copies

        def waves(it, halo_copies, mode_copies, trades):
            core_copies = {}

            def to_core(d, what):
                core_copies[d] = send(
                    grad.at[it, what, theirs, :], land_core.at[it, what], s_core.at[it, d], r_core.at[it, d], other
                )

            def pass_on(d):
                if d not in trades:
                    for copies in mode_copies:
                        copies[d].wait_recv()
                    trades[d] = trade(it, d)

            if it == 0:
                for d in arrival:
                    pass_on(d)
            for copy in halo_copies:
                copy.wait_recv()
            take_patches(it)
            to_core(n_mode, pl.ds(planes, 1))
            if 0 in trades:
                trades[0].wait_recv()
            forward(it, 0)
            for i, d in enumerate(arrival):
                pass_on(d)
                if i + 1 < len(arrival):
                    pass_on(arrival[i + 1])
                trades[d].wait_recv()
                forward(it, d)
            set_factors()
            down = weight_down(it)
            core_copies[n_mode].wait_recv()
            density = grad[it, planes, mine, :] + land_core[it, planes]
            mode_sums = {}

            def fold(d):
                k = mode_of(d)
                core_copies[d].wait_recv()
                for c in range(2):
                    acc_core[it, k, c] = grad[it, 2 * k + c, mine, :] + land_core[it, 2 * k + c]
                acc_core[it, k, 2] = density
                if d > 0:
                    for e in far_first:
                        where = pl.ds(pl.multiple_of(flipped(block_of(it), e) * wide, wide), wide)
                        mode_sums[d, e] = send(
                            acc_core.at[it, k, :, where, :], land_x.at[it, d - 1, :, where, :],
                            s_x.at[it, d - 1, e], r_x.at[it, d - 1, e], near(0, n_mode - d),
                        )

            order = list(range(1, n_mode)) + [0]
            for i, d in enumerate(order):
                backward(it, d, i == 0)
                to_core(d, pl.ds(2 * mode_of(d), 2))
                if i > 0:
                    fold(order[i - 1])
            down = down + terms_down(it)
            fold(0)
            return mode_sums, down

        def reduce_steps(it, mode_sums, mode_copies, trades):
            last = it == ITERS - 1
            split_rings = SPLIT_RINGS[it]
            a = ring_of(it)
            b = y + z - a

            def at(first, second):
                if split_rings:
                    yy = second * (1 - core) + first * core
                    zz = first * (1 - core) + second * core
                else:
                    yy, zz = second, first
                return ((zz * side + yy) * CORES + core, m)

            peers_b = [at(a, lax.rem(b + d, side)) for d in range(1, side)]
            ring = {}
            for e in far_first:
                where = pl.ds(pl.multiple_of(flipped(block_of(it), e) * wide, wide), wide)
                for d in range(1, n_mode):
                    mode_sums[d, e].wait_recv()
                for c in range(3):
                    total = acc_core[it, m, c, where, :]
                    for d in range(1, n_mode):
                        total = total + land_x[it, d - 1, c, where, :]
                    acc_x[it, c, where, :] = total
                for g in (2 * e, 2 * e + 1):
                    if g > 0:
                        t = flipped(a, g)
                        ring[g] = send(
                            acc_x.at[it, :, pl.ds(pl.multiple_of(t * rows, rows), rows), :], land_ring.at[it, g - 1],
                            s_ring.at[it, g - 1], r_ring.at[it, g - 1], at(t, b),
                        )
            yield
            total = acc_x[it, :, pl.ds(pl.multiple_of(a * rows, rows), rows), :]
            for g in range(1, side):
                ring[g].wait_recv()
                total = total + land_ring[it, g - 1]
            all_b[it, b] = total
            copies = [
                send(all_b.at[it, b], all_b.at[it, b], s_all.at[it, i], r_all.at[it, i], device)
                for i, device in enumerate(peers_b)
            ]
            yield
            for copy in copies:
                copy.wait_recv()
            total = all_b[it, 0]
            for i in range(1, side):
                total = total + all_b[it, i]
            spot = pl.ds(pl.multiple_of(core * half + a * rows, rows), rows)
            probes[it + 1, own_mode, spot, :] = probes[it, own_mode, spot, :] + total[0:2] / (total[2:3] + 1.0)
            piece = probes.at[it + 1, own_mode, spot, :]
            ring = {
                g: send(piece, piece, s_gather.at[it, g - 1], r_gather.at[it, g - 1], at(flipped(a, g), b))
                for g in range(side - 1, 0, -1)
            }
            yield
            for e in sorted(range(pairs), key=lambda e: (e == pairs // 2 and e > 0, e)):
                for g in (2 * e, 2 * e + 1):
                    if g > 0:
                        ring[g].wait_recv()
                if not last:
                    first_row = core * half + flipped(block_of(it), e) * wide
                    mode_copies.append(send_mode(it + 1, e, pl.ds(pl.multiple_of(first_row, wide), wide)))
            trades[0] = trade(it + 1, 0)
            if last:
                trades[0].wait_recv()
            yield

        def with_above(it, own, landed):
            for i in range(2):
                own = own + jnp.where(s > i, landed(i), 0.0)
            return own

        def weight_beside(it, down):
            for copy in down[:2]:
                copy.wait_recv()
            for c in range(3):
                folded[it, c, 2] = with_above(it, sums[it, c, 2, 0:tile, :], lambda i: land_weight[it, i, c])
            return send(folded.at[it, 2, 2], land_beside.at[it, 2], s_beside.at[it, 0], r_beside.at[it, 0], after[2])

        def terms_beside(it, down):
            for copy in down[2:4]:
                copy.wait_recv()
            for p in range(2):
                folded[it, 2, p] = with_above(it, sums[it, 2, p, 0:tile, :], lambda i: land_edge[it, i, p])
            return send(folded.at[it, 2, pl.ds(0, 2)], land_beside.at[it, pl.ds(0, 2)],
                        s_beside.at[it, 1], r_beside.at[it, 1], after[2])

        def new_object(it, copies):
            for copy in copies:
                copy.wait_recv()
            for c in range(2):
                terms = []
                for p in range(3):
                    if p == 2:
                        term = folded[it, c, 2]
                    else:
                        term = with_above(it, sums[it, c, p, 0:tile, :], lambda i: land_down[it, i, c, p])
                    if c == 0:
                        term = term + jnp.where(m > 0, land_beside[it, p], 0.0)
                    terms.append(term)
                for p in range(2):
                    fresh = ext[it, p, c, 0:tile, :] + terms[p] / (terms[2] + 1.0)
                    if it == ITERS - 1:
                        obj_out[p, :, c * N : (c + 1) * N] = fresh
                    else:
                        ext[it + 1, p, c, 0:tile, :] = fresh

        for copy in fetched[3:]:
            copy.wait()
        for it in range(ITERS):
            mode_sums, down = waves(it, halo_copies, probe_copies, trades)
            probe_copies, trades = [], {}
            steps = reduce_steps(it, mode_sums, probe_copies, trades)
            beside = [weight_beside(it, down)]
            next(steps)
            beside.append(terms_beside(it, down))
            next(steps)
            new_object(it, beside + down[4:])
            if it + 1 < ITERS:
                halo_copies = start_halo(it + 1)
            next(steps)
            next(steps)
        probe_out[0] = probes[ITERS, own_mode]
        for copy in started:
            copy.wait_send()

    return kernel


def scratch_of(plan):
    n_mode, side, tile = plan.n_mode, plan.side, plan.tile
    planes, half, rows = plan.planes, plan.half, plan.rows

    def vmem(*shape, kind=F32):
        return pltpu.VMEM(shape, kind)

    def sems(*shape):
        return [pltpu.SemaphoreType.DMA(shape), pltpu.SemaphoreType.DMA(shape)]

    return [
        vmem(ITERS, 2, 3, 3 * tile, N),
        vmem(ITERS + 1, planes, N, N),
        vmem(2, N, N),
        vmem(2, 2 * N, 2 * N, kind=BF16),
        vmem(2, 2 * N, 2 * N, kind=BF16),
        vmem(ITERS, 3, 3, 3 * tile, N),
        vmem(2, 3, 4, 256, N),
        vmem(2, 2, N, N),
        vmem(n_mode, 2 * N, 2 * N),
        vmem(n_mode, 2 * N, 2 * N, kind=BF16),
        vmem(n_mode, 2 * N, 2 * N, kind=BF16),
        vmem(n_mode, 2 * N, 2 * N, kind=BF16),
        vmem(n_mode, 2 * N, 2 * N, kind=BF16),
        vmem(n_mode, 2 * N, 2 * N),
        vmem(2, N, N),
        vmem(2, 2, N, N),
        vmem(ITERS, planes + 1, N, N),
        vmem(ITERS, planes + 1, half, N),
        vmem(ITERS, n_mode, 3, half, N),
        vmem(ITERS, n_mode - 1, 3, half, N),
        vmem(ITERS, 3, half, N),
        vmem(ITERS, side - 1, 3, rows, N),
        vmem(ITERS, side, 3, rows, N),
        vmem(ITERS, 2, 3, tile, N),
        vmem(ITERS, 2, 2, tile, N),
        vmem(ITERS, 2, 2, 2, tile, N),
        vmem(ITERS, 3, 3, tile, N),
        vmem(ITERS, 3, tile, N),
        pltpu.SemaphoreType.DMA((6,)),
        *sems(ITERS, n_mode, side // 2),
        *sems(ITERS + 1, n_mode),
        *sems(ITERS, 5),
        *sems(ITERS, 2),
        *sems(ITERS, 4),
        *sems(ITERS, 2),
        *sems(ITERS, n_mode + 1),
        *sems(ITERS, n_mode - 1, side // 2),
        *sems(ITERS, side - 1),
        *sems(ITERS, side - 1),
        *sems(ITERS, side - 1),
    ]


def solution(mesh):
    n_scan, n_mode = mesh.shape["scan"], mesh.shape["mode"]
    left_np, right_np = fresnel_blocks()

    def local(object_field, probe, amplitude, offsets, counts):
        plan = Plan(n_scan, n_mode, object_field.shape[1])
        in_vmem = pl.BlockSpec(memory_space=pltpu.VMEM)
        in_smem = pl.BlockSpec(memory_space=pltpu.SMEM)
        return pl.pallas_call(
            make_kernel(plan),
            out_shape=(
                jax.ShapeDtypeStruct(object_field.shape, F32),
                jax.ShapeDtypeStruct(probe.shape, F32),
            ),
            in_specs=[pl.BlockSpec(memory_space=pltpu.HBM)] * 5 + [in_smem] * 2,
            out_specs=(in_vmem, in_vmem),
            scratch_shapes=scratch_of(plan),
            compiler_params=pltpu.CompilerParams(
                collective_id=0, has_side_effects=True, vmem_limit_bytes=60 * 1024 * 1024
            ),
        )(object_field, probe, amplitude, jnp.asarray(left_np), jnp.asarray(right_np), offsets, counts)

    placed = (
        P(None, "scan", "mode"),
        P("mode", None, None, None),
        P(("scan", "mode"), None, None),
        P(("scan", "mode"), None),
        P(("scan", "mode")),
    )
    return jax.shard_map(
        local,
        mesh=mesh,
        in_specs=placed,
        out_specs=(P(None, "scan", "mode"), P("mode", None, None, None)),
        check_vma=False,
    )
```

```python
import math

import jax
import jax.numpy as jnp
import ml_dtypes
import numpy as np
from jax import lax
from jax.experimental import pallas as pl
from jax.experimental.pallas import tpu as pltpu
from jax.sharding import PartitionSpec as P

ITERS = 2
CORES = 2
N = 128
SPLIT_RINGS = (True, True)
MESH = pl.DeviceIdType.MESH
F32 = jnp.float32
BF16 = jnp.bfloat16


def fresnel_blocks():
    ids = np.arange(N)
    phase = (ids[:, None] * ids[None, :]) % N
    chirp = ((ids - N // 2) ** 2) % (4 * N)
    angle = -2.0 * math.pi / N * phase + math.pi / (2 * N) * chirp[None, :]
    re, im = np.cos(angle) / math.sqrt(N), np.sin(angle) / math.sqrt(N)
    full = np.block([[re, -im], [im, re]]).astype(np.float32)

    def parts(matrix):
        high = matrix.astype(ml_dtypes.bfloat16)
        low = (matrix - high.astype(np.float32)).astype(ml_dtypes.bfloat16)
        return np.stack([high, low])

    return parts(full), parts(np.ascontiguousarray(full.T))


def split(value):
    high = value.astype(BF16)
    return high, (value - high.astype(F32)).astype(BF16)


def dot(first, second):
    return jnp.dot(first, second, preferred_element_type=F32)


def dot3(first_high, first_low, second_high, second_low):
    return dot(first_high, second_high) + dot(first_high, second_low) + dot(first_low, second_high)


class Plan:
    def __init__(self, n_scan, n_mode, tile_rows):
        self.n_scan, self.n_mode, self.tile = n_scan, n_mode, tile_rows
        self.side = math.isqrt(n_scan // CORES)
        assert self.side * self.side * CORES == n_scan
        self.planes = 2 * n_mode
        self.half = N // CORES
        self.rows = self.half // self.side


def make_kernel(plan):
    n_scan, n_mode, tile, side = plan.n_scan, plan.n_mode, plan.tile, plan.side
    planes, half, rows = plan.planes, plan.half, plan.rows
    far_rows = n_scan * tile
    far_cols = n_mode * 2 * N

    def kernel(
        obj_hbm, probe_hbm, amp_hbm, left_hbm, right_hbm, off_ref, cnt_ref,
        obj_out, probe_out,
        obj_new, ext, probes, amp_ref, left_ref, right_ref, sums, pad, patch, exits, ah, al, xh, xl, far, factor, num,
        grad, land_core, acc_core, density_sum, land_x, acc_x, land_ring, all_b,
        land_weight, land_edge, land_down, folded, land_beside,
        s_in, s_probe, r_probe, s_fwd, r_fwd, s_halo, r_halo, s_weight, r_weight, s_down, r_down, s_beside, r_beside,
        s_core, r_core, s_density, r_density, s_x, r_x, s_ring, r_ring, s_all, r_all,
        s_gather, r_gather,
    ):
        s = lax.axis_index("scan")
        m = lax.axis_index("mode")
        core = lax.rem(s, CORES)
        chip = lax.div(s, CORES)
        y, z = lax.rem(chip, side), lax.div(chip, side)
        other = (s + 1 - 2 * core, m)

        def near(ds, dm):
            return (lax.rem(s + ds + n_scan, n_scan), lax.rem(m + dm + n_mode, n_mode))

        ring_y = [((z * side + lax.rem(y + d, side)) * CORES + core, m) for d in range(1, side)]
        ring_z = [((lax.rem(z + d, side) * side + y) * CORES + core, m) for d in range(1, side)]
        peers_x = [near(0, d) for d in range(1, n_mode)]
        halo_steps = [(1, 0), (2, 0), (0, 1), (1, 1), (2, 1)]
        before = [near(-ds, -dm) for ds, dm in halo_steps]
        after = [near(ds, dm) for ds, dm in halo_steps]
        peers = [other] + ring_y + ring_z + peers_x + before + after

        started = []
        settled = []

        def settle(upto):
            while len(settled) < upto:
                started[len(settled)].wait_send()
                settled.append(True)

        def send(src, dst, send_sem, recv_sem, device):
            copy = pltpu.make_async_remote_copy(
                src_ref=src, dst_ref=dst, send_sem=send_sem, recv_sem=recv_sem,
                device_id=device, device_id_type=MESH,
            )
            copy.start()
            started.append(copy)
            return copy

        barrier = pltpu.get_barrier_semaphore()
        for device in peers:
            pl.semaphore_signal(barrier, inc=1, device_id=device, device_id_type=MESH)

        fetched = [
            pltpu.make_async_copy(obj_hbm.at[:, :, pl.ds(0, N)], ext.at[0, :, 0, pl.ds(0, tile), :], s_in.at[0]),
            pltpu.make_async_copy(obj_hbm.at[:, :, pl.ds(N, N)], ext.at[0, :, 1, pl.ds(0, tile), :], s_in.at[1]),
            pltpu.make_async_copy(probe_hbm.at[0], probes.at[0, pl.ds(2 * m, 2)], s_in.at[2]),
            pltpu.make_async_copy(right_hbm, right_ref, s_in.at[3]),
            pltpu.make_async_copy(left_hbm, left_ref, s_in.at[4]),
            pltpu.make_async_copy(amp_hbm, amp_ref, s_in.at[5]),
        ]
        for copy in fetched:
            copy.start()
        for copy in fetched[:3]:
            copy.wait()
        pl.semaphore_wait(barrier, len(peers))

        def start_halo(it):
            copies = []
            for i in (1, 2):
                copies.append(
                    send(ext.at[it, :, pl.ds(0, 2), pl.ds(0, tile), :],
                         ext.at[it, :, pl.ds(0, 2), pl.ds(i * tile, tile), :],
                         s_halo.at[it, i - 1], r_halo.at[it, i - 1], before[i - 1])
                )
            for i in range(3):
                copies.append(
                    send(ext.at[it, :, 0, pl.ds(0, tile), :],
                         ext.at[it, :, 2, pl.ds(i * tile, tile), :],
                         s_halo.at[it, 2 + i], r_halo.at[it, 2 + i], before[2 + i])
                )
            return copies

        mine = pl.ds(core * half, half)
        theirs = pl.ds((1 - core) * half, half)
        own_mode = pl.ds(2 * m, 2)
        arrival = [d for d in range(1, n_mode) if d != n_mode // 2] + [n_mode // 2]

        pairs = side // 2
        wide = 2 * rows

        def flipped(value, mask):
            out, bit = value, 1
            while bit <= mask:
                if mask & bit:
                    out = out + bit - 2 * bit * lax.rem(lax.div(value, bit), 2)
                bit *= 2
            return out

        far_first = sorted(range(pairs), key=lambda e: (e != pairs // 2, e == 0, e))

        def ring_of(it):
            return y * core + z * (1 - core) if SPLIT_RINGS[it] else z

        def block_of(it):
            return lax.div(ring_of(it), 2)

        def mode_of(d):
            return lax.rem(m - d + n_mode, n_mode)

        def send_mode(it, e, where):
            piece = probes.at[it, own_mode, where, :]
            return {d: send(piece, piece, s_probe.at[it, d, e], r_probe.at[it, d, e], near(0, d)) for d in arrival}

        def trade(it, d):
            piece = probes.at[it, pl.ds(2 * mode_of(d), 2), mine, :]
            return send(piece, piece, s_fwd.at[it, d], r_fwd.at[it, d], other)

        probe_copies = [send_mode(0, 0, mine)]
        halo_copies = start_halo(0)
        trades = {}
        zero_half = jnp.zeros((64, N), F32)
        zero_block = jnp.zeros((256, N), F32)
        for j in range(2):
            for p in range(3):
                pad[j, p, 0] = zero_block
                pad[j, p, 3] = zero_block
                for c in (1, 2):
                    pad[j, p, c, 0:64, :] = zero_half
                    pad[j, p, c, 192:256, :] = zero_half

        lane = lax.broadcasted_iota(jnp.int32, (N, N), 1)
        row_id = lax.broadcasted_iota(jnp.int32, (N, N), 0)

        def used_of(j):
            return jnp.where(j < cnt_ref[0], 1.0, 0.0).astype(F32)

        def spot_of(j):
            row, col = lax.rem(off_ref[j, 0], tile), lax.rem(off_ref[j, 1], 2 * N)
            return row, lax.div(col, N), lax.rem(col, N)

        def take_patches(it):
            density = jnp.zeros((N, N), F32)
            for j in range(2):
                row, col_block, col_lane = spot_of(j)
                inside = (row_id + off_ref[j, 0] < far_rows) & (lane + off_ref[j, 1] < far_cols)
                for p in range(2):
                    one = ext[it, p, col_block, pl.ds(row, N), :]
                    two = ext[it, p, col_block + 1, pl.ds(row, N), :]
                    moved = pltpu.roll(jnp.where(lane >= col_lane, one, two), lax.rem(N - col_lane, N), 1)
                    moved = jnp.where(inside, moved, 0.0)
                    patch[j, p] = moved
                    density = density + moved * moved * used_of(j)
            grad[it, planes] = density

        def forward(it, d):
            k = mode_of(d)
            pr, pi = probes[it, 2 * k], probes[it, 2 * k + 1]
            for j in range(2):
                rows_j = pl.ds(j * N, N)
                o_re, o_im = patch[j, 0], patch[j, 1]
                for c, value in ((0, pr * o_re - pi * o_im), (1, pr * o_im + pi * o_re)):
                    cols_c = pl.ds(c * N, N)
                    exits[d, rows_j, cols_c] = value
                    high, low = split(value)
                    ah[d, rows_j, cols_c] = high
                    al[d, rows_j, cols_c] = low
            high, low = split(dot3(ah[d], al[d], right_ref[0], right_ref[1]))
            for j in range(2):
                for c in range(2):
                    block = (slice(j * N, (j + 1) * N), slice(c * N, (c + 1) * N))
                    xh[d, pl.ds(c * N, N), pl.ds(j * N, N)] = high[block]
                    xl[d, pl.ds(c * N, N), pl.ds(j * N, N)] = low[block]
            far[d] = dot3(left_ref[0], left_ref[1], xh[d], xl[d])

        def set_factors():
            for j in range(2):
                intensity = jnp.zeros((N, N), F32)
                for d in range(n_mode):
                    for c in range(2):
                        part = far[d, pl.ds(c * N, N), pl.ds(j * N, N)]
                        intensity = intensity + part * part
                factor[j] = amp_ref[j] / jnp.sqrt(jnp.maximum(intensity, 1.0))

        def backward(it, d, first):
            k = mode_of(d)
            for j in range(2):
                for c in range(2):
                    block = (pl.ds(c * N, N), pl.ds(j * N, N))
                    high, low = split(far[(d,) + block] * factor[j])
                    xh[(d,) + block] = high
                    xl[(d,) + block] = low
            high, low = split(dot3(right_ref[0], right_ref[1], xh[d], xl[d]))
            for j in range(2):
                for c in range(2):
                    block = (slice(c * N, (c + 1) * N), slice(j * N, (j + 1) * N))
                    ah[d, pl.ds(j * N, N), pl.ds(c * N, N)] = high[block]
                    al[d, pl.ds(j * N, N), pl.ds(c * N, N)] = low[block]
            change = dot3(ah[d], al[d], left_ref[0], left_ref[1]) - exits[d]
            pr, pi = probes[it, 2 * k], probes[it, 2 * k + 1]
            g_re = jnp.zeros((N, N), F32)
            g_im = jnp.zeros((N, N), F32)
            for j in range(2):
                c_re = change[j * N : (j + 1) * N, 0:N]
                c_im = change[j * N : (j + 1) * N, N : 2 * N]
                o_re, o_im = patch[j, 0] * used_of(j), patch[j, 1] * used_of(j)
                g_re = g_re + (o_re * c_re + o_im * c_im)
                g_im = g_im + (o_re * c_im - o_im * c_re)
                n_re = pr * c_re + pi * c_im
                n_im = pr * c_im - pi * c_re
                if first:
                    num[j, 0] = n_re
                    num[j, 1] = n_im
                else:
                    num[j, 0] += n_re
                    num[j, 1] += n_im
            grad[it, 2 * k] = g_re
            grad[it, 2 * k + 1] = g_im

        def set_pad(j, p, value):
            _, _, col_lane = spot_of(j)
            moved = pltpu.roll(value * used_of(j), col_lane, 1)
            pad[j, p, 1, 64:192, :] = jnp.where(lane >= col_lane, moved, 0.0)
            pad[j, p, 2, 64:192, :] = jnp.where(lane < col_lane, moved, 0.0)

        def placed(p, c):
            row_0, block_0, _ = spot_of(0)
            row_1, block_1, _ = spot_of(1)
            return (
                pad[0, p, c + 1 - block_0, pl.ds(64 - row_0, 192), :]
                + pad[1, p, c + 1 - block_1, pl.ds(64 - row_1, 192), :]
            )

        def weight_down(it):
            weight = jnp.zeros((N, N), F32)
            for p in range(planes):
                weight = weight + probes[it, p] * probes[it, p]
            for j in range(2):
                set_pad(j, 2, weight)
            for c in range(3):
                sums[it, c, 2] = placed(2, c)
            return [
                send(sums.at[it, :, 2, pl.ds(i * tile, tile), :], land_weight.at[it, i - 1],
                     s_weight.at[it, i - 1], r_weight.at[it, i - 1], after[i - 1])
                for i in (1, 2)
            ]

        def terms_down(it):
            for j in range(2):
                for p in range(2):
                    set_pad(j, p, num[j, p])
            copies = []
            for p in range(2):
                sums[it, 2, p] = placed(p, 2)
            for i in (1, 2):
                copies.append(
                    send(sums.at[it, 2, pl.ds(0, 2), pl.ds(i * tile, tile), :], land_edge.at[it, i - 1],
                         s_down.at[it, i - 1], r_down.at[it, i - 1], after[i - 1])
                )
            for c in range(2):
                for p in range(2):
                    sums[it, c, p] = placed(p, c)
            for i in (1, 2):
                copies.append(
                    send(sums.at[it, pl.ds(0, 2), pl.ds(0, 2), pl.ds(i * tile, tile), :], land_down.at[it, i - 1],
                         s_down.at[it, i + 1], r_down.at[it, i + 1], after[i - 1])
                )
            return copies

        def waves(it, halo_copies, mode_copies, trades):
            core_copies = {}

            def to_core(d, what):
                core_copies[d] = send(
                    grad.at[it, what, theirs, :], land_core.at[it, what], s_core.at[it, d], r_core.at[it, d], other
                )

            def pass_on(d):
                if d not in trades:
                    for copies in mode_copies:
                        copies[d].wait_recv()
                    trades[d] = trade(it, d)

            if it == 0:
                for d in arrival:
                    pass_on(d)
            for copy in halo_copies:
                copy.wait_recv()
            take_patches(it)
            to_core(n_mode, pl.ds(planes, 1))
            if 0 in trades:
                trades[0].wait_recv()
            forward(it, 0)
            for i, d in enumerate(arrival):
                pass_on(d)
                if i + 1 < len(arrival):
                    pass_on(arrival[i + 1])
                trades[d].wait_recv()
                forward(it, d)
            core_copies[n_mode].wait_recv()
            density_sum[it, 0] = grad[it, planes, mine, :] + land_core[it, planes]
            mode_sums = {}
            for d in range(1, n_mode):
                mode_sums[d] = send(density_sum.at[it, 0], density_sum.at[it, d],
                                    s_density.at[it, d - 1], r_density.at[it, d - 1], near(0, d))
            set_factors()
            down = weight_down(it)

            def fold(d):
                k = mode_of(d)
                core_copies[d].wait_recv()
                for c in range(2):
                    acc_core[it, k, c] = grad[it, 2 * k + c, mine, :] + land_core[it, 2 * k + c]
                if d > 0:
                    for e in far_first:
                        where = pl.ds(pl.multiple_of(flipped(block_of(it), e) * wide, wide), wide)
                        mode_sums[d, e] = send(
                            acc_core.at[it, k, :, where, :], land_x.at[it, d - 1, :, where, :],
                            s_x.at[it, d - 1, e], r_x.at[it, d - 1, e], near(0, n_mode - d),
                        )

            order = arrival[::-1] + [0]
            for i, d in enumerate(order):
                backward(it, d, i == 0)
                to_core(d, pl.ds(2 * mode_of(d), 2))
                if i > 0:
                    fold(order[i - 1])
            down = down + terms_down(it)
            fold(0)
            return mode_sums, down

        def reduce_steps(it, mode_sums, mode_copies, trades):
            last = it == ITERS - 1
            split_rings = SPLIT_RINGS[it]
            a = ring_of(it)
            b = y + z - a

            def at(first, second):
                if split_rings:
                    yy = second * (1 - core) + first * core
                    zz = first * (1 - core) + second * core
                else:
                    yy, zz = second, first
                return ((zz * side + yy) * CORES + core, m)

            peers_b = [at(a, lax.rem(b + d, side)) for d in range(1, side)]
            ring = {}
            total = density_sum[it, 0]
            for d in range(1, n_mode):
                mode_sums[d].wait_recv()
                total = total + density_sum[it, d]
            acc_x[it, 2] = total
            for e in far_first:
                where = pl.ds(pl.multiple_of(flipped(block_of(it), e) * wide, wide), wide)
                for d in range(1, n_mode):
                    mode_sums[d, e].wait_recv()
                for c in range(2):
                    total = acc_core[it, m, c, where, :]
                    for d in range(1, n_mode):
                        total = total + land_x[it, d - 1, c, where, :]
                    acc_x[it, c, where, :] = total
                for g in (2 * e, 2 * e + 1):
                    if g > 0:
                        t = flipped(a, g)
                        ring[g] = send(
                            acc_x.at[it, :, pl.ds(pl.multiple_of(t * rows, rows), rows), :], land_ring.at[it, g - 1],
                            s_ring.at[it, g - 1], r_ring.at[it, g - 1], at(t, b),
                        )
            yield
            total = acc_x[it, :, pl.ds(pl.multiple_of(a * rows, rows), rows), :]
            for g in range(1, side):
                ring[g].wait_recv()
                total = total + land_ring[it, g - 1]
            all_b[it, b] = total
            copies = [
                send(all_b.at[it, b], all_b.at[it, b], s_all.at[it, i], r_all.at[it, i], device)
                for i, device in enumerate(peers_b)
            ]
            yield
            for copy in copies:
                copy.wait_recv()
            total = all_b[it, 0]
            for i in range(1, side):
                total = total + all_b[it, i]
            spot = pl.ds(pl.multiple_of(core * half + a * rows, rows), rows)
            probes[it + 1, own_mode, spot, :] = probes[it, own_mode, spot, :] + total[0:2] / (total[2:3] + 1.0)
            piece = probes.at[it + 1, own_mode, spot, :]
            ring = {
                g: send(piece, piece, s_gather.at[it, g - 1], r_gather.at[it, g - 1], at(flipped(a, g), b))
                for g in range(side - 1, 0, -1)
            }
            yield
            for e in sorted(range(pairs), key=lambda e: (e == pairs // 2 and e > 0, e)):
                for g in (2 * e, 2 * e + 1):
                    if g > 0:
                        ring[g].wait_recv()
                if not last:
                    first_row = core * half + flipped(block_of(it), e) * wide
                    mode_copies.append(send_mode(it + 1, e, pl.ds(pl.multiple_of(first_row, wide), wide)))
            trades[0] = trade(it + 1, 0)
            if last:
                trades[0].wait_recv()
            yield

        def with_above(it, own, landed):
            for i in range(2):
                own = own + jnp.where(s > i, landed(i), 0.0)
            return own

        def weight_beside(it, down):
            for copy in down[:2]:
                copy.wait_recv()
            for c in range(3):
                folded[it, c, 2] = with_above(it, sums[it, c, 2, 0:tile, :], lambda i: land_weight[it, i, c])
            return send(folded.at[it, 2, 2], land_beside.at[it, 2], s_beside.at[it, 0], r_beside.at[it, 0], after[2])

        def terms_beside(it, down):
            for copy in down[2:4]:
                copy.wait_recv()
            for p in range(2):
                folded[it, 2, p] = with_above(it, sums[it, 2, p, 0:tile, :], lambda i: land_edge[it, i, p])
            return send(folded.at[it, 2, pl.ds(0, 2)], land_beside.at[it, pl.ds(0, 2)],
                        s_beside.at[it, 1], r_beside.at[it, 1], after[2])

        def new_object(it, copies):
            for copy in copies:
                copy.wait_recv()
            for c in range(2):
                terms = []
                for p in range(3):
                    if p == 2:
                        term = folded[it, c, 2]
                    else:
                        term = with_above(it, sums[it, c, p, 0:tile, :], lambda i: land_down[it, i, c, p])
                    if c == 0:
                        term = term + jnp.where(m > 0, land_beside[it, p], 0.0)
                    terms.append(term)
                for p in range(2):
                    fresh = ext[it, p, c, 0:tile, :] + terms[p] / (terms[2] + 1.0)
                    if it == ITERS - 1:
                        obj_new[p, :, c * N : (c + 1) * N] = fresh
                    else:
                        ext[it + 1, p, c, 0:tile, :] = fresh

        for copy in fetched[3:]:
            copy.wait()
        out_copies = []
        for it in range(ITERS):
            early = len(started)
            mode_sums, down = waves(it, halo_copies, probe_copies, trades)
            probe_copies, trades = [], {}
            steps = reduce_steps(it, mode_sums, probe_copies, trades)
            beside = [weight_beside(it, down)]
            next(steps)
            beside.append(terms_beside(it, down))
            next(steps)
            if it + 1 < ITERS:
                new_object(it, beside + down[4:])
                halo_copies = start_halo(it + 1)
            next(steps)
            if it + 1 == ITERS:
                new_object(it, beside + down[4:])
            settle(early)
            if it == ITERS - 1:
                out_copies.append(pltpu.make_async_copy(obj_new, obj_out, s_in.at[0]))
                out_copies[0].start()
                settle(len(started) - 2 * side)
            next(steps)
        out_copies.append(pltpu.make_async_copy(probes.at[ITERS, own_mode], probe_out.at[0], s_in.at[1]))
        out_copies[1].start()
        settle(len(started))
        for copy in out_copies:
            copy.wait()

    return kernel


def scratch_of(plan):
    n_mode, side, tile = plan.n_mode, plan.side, plan.tile
    planes, half, rows = plan.planes, plan.half, plan.rows

    def vmem(*shape, kind=F32):
        return pltpu.VMEM(shape, kind)

    def sems(*shape):
        return [pltpu.SemaphoreType.DMA(shape), pltpu.SemaphoreType.DMA(shape)]

    return [
        vmem(2, tile, 2 * N),
        vmem(ITERS, 2, 3, 3 * tile, N),
        vmem(ITERS + 1, planes, N, N),
        vmem(2, N, N),
        vmem(2, 2 * N, 2 * N, kind=BF16),
        vmem(2, 2 * N, 2 * N, kind=BF16),
        vmem(ITERS, 3, 3, 3 * tile, N),
        vmem(2, 3, 4, 256, N),
        vmem(2, 2, N, N),
        vmem(n_mode, 2 * N, 2 * N),
        vmem(n_mode, 2 * N, 2 * N, kind=BF16),
        vmem(n_mode, 2 * N, 2 * N, kind=BF16),
        vmem(n_mode, 2 * N, 2 * N, kind=BF16),
        vmem(n_mode, 2 * N, 2 * N, kind=BF16),
        vmem(n_mode, 2 * N, 2 * N),
        vmem(2, N, N),
        vmem(2, 2, N, N),
        vmem(ITERS, planes + 1, N, N),
        vmem(ITERS, planes + 1, half, N),
        vmem(ITERS, n_mode, 2, half, N),
        vmem(ITERS, n_mode, half, N),
        vmem(ITERS, n_mode - 1, 2, half, N),
        vmem(ITERS, 3, half, N),
        vmem(ITERS, side - 1, 3, rows, N),
        vmem(ITERS, side, 3, rows, N),
        vmem(ITERS, 2, 3, tile, N),
        vmem(ITERS, 2, 2, tile, N),
        vmem(ITERS, 2, 2, 2, tile, N),
        vmem(ITERS, 3, 3, tile, N),
        vmem(ITERS, 3, tile, N),
        pltpu.SemaphoreType.DMA((6,)),
        *sems(ITERS, n_mode, side // 2),
        *sems(ITERS + 1, n_mode),
        *sems(ITERS, 5),
        *sems(ITERS, 2),
        *sems(ITERS, 4),
        *sems(ITERS, 2),
        *sems(ITERS, n_mode + 1),
        *sems(ITERS, n_mode - 1),
        *sems(ITERS, n_mode - 1, side // 2),
        *sems(ITERS, side - 1),
        *sems(ITERS, side - 1),
        *sems(ITERS, side - 1),
    ]


def solution(mesh):
    n_scan, n_mode = mesh.shape["scan"], mesh.shape["mode"]
    left_np, right_np = fresnel_blocks()

    def local(object_field, probe, amplitude, offsets, counts):
        plan = Plan(n_scan, n_mode, object_field.shape[1])
        in_smem = pl.BlockSpec(memory_space=pltpu.SMEM)
        return pl.pallas_call(
            make_kernel(plan),
            out_shape=(
                jax.ShapeDtypeStruct(object_field.shape, F32),
                jax.ShapeDtypeStruct(probe.shape, F32),
            ),
            in_specs=[pl.BlockSpec(memory_space=pltpu.HBM)] * 5 + [in_smem] * 2,
            out_specs=(pl.BlockSpec(memory_space=pltpu.HBM),) * 2,
            scratch_shapes=scratch_of(plan),
            compiler_params=pltpu.CompilerParams(
                collective_id=0, has_side_effects=True, vmem_limit_bytes=60 * 1024 * 1024
            ),
        )(object_field, probe, amplitude, jnp.asarray(left_np), jnp.asarray(right_np), offsets, counts)

    placed = (
        P(None, "scan", "mode"),
        P("mode", None, None, None),
        P(("scan", "mode"), None, None),
        P(("scan", "mode"), None),
        P(("scan", "mode")),
    )
    return jax.shard_map(
        local,
        mesh=mesh,
        in_specs=placed,
        out_specs=(P(None, "scan", "mode"), P("mode", None, None, None)),
        check_vma=False,
    )
```

```python
import math

import jax
import jax.numpy as jnp
import ml_dtypes
import numpy as np
from jax import lax
from jax.experimental import pallas as pl
from jax.experimental.pallas import tpu as pltpu
from jax.sharding import PartitionSpec as P

ITERS = 2
CORES = 2
N = 128
SPLIT_RINGS = (True, True)
MESH = pl.DeviceIdType.MESH
F32 = jnp.float32
BF16 = jnp.bfloat16


def fresnel_blocks():
    ids = np.arange(N)
    phase = (ids[:, None] * ids[None, :]) % N
    chirp = ((ids - N // 2) ** 2) % (4 * N)
    angle = -2.0 * math.pi / N * phase + math.pi / (2 * N) * chirp[None, :]
    re, im = np.cos(angle) / math.sqrt(N), np.sin(angle) / math.sqrt(N)
    full = np.block([[re, -im], [im, re]]).astype(np.float32)

    def parts(matrix):
        high = matrix.astype(ml_dtypes.bfloat16)
        low = (matrix - high.astype(np.float32)).astype(ml_dtypes.bfloat16)
        return np.stack([high, low])

    return parts(full), parts(np.ascontiguousarray(full.T))


def split(value):
    high = value.astype(BF16)
    return high, (value - high.astype(F32)).astype(BF16)


def dot(first, second):
    return jnp.dot(first, second, preferred_element_type=F32)


def dot3(first_high, first_low, second_high, second_low):
    return dot(first_high, second_high) + dot(first_high, second_low) + dot(first_low, second_high)


class Plan:
    def __init__(self, n_scan, n_mode, tile_rows):
        self.n_scan, self.n_mode, self.tile = n_scan, n_mode, tile_rows
        self.side = math.isqrt(n_scan // CORES)
        assert self.side * self.side * CORES == n_scan
        self.planes = 2 * n_mode
        self.half = N // CORES
        self.rows = self.half // self.side


def make_kernel(plan):
    n_scan, n_mode, tile, side = plan.n_scan, plan.n_mode, plan.tile, plan.side
    planes, half, rows = plan.planes, plan.half, plan.rows
    far_rows = n_scan * tile
    far_cols = n_mode * 2 * N

    def kernel(
        obj_hbm, probe_hbm, amp_hbm, left_hbm, right_hbm, off_ref, cnt_ref,
        obj_out, probe_out,
        obj_new, ext, probes, amp_ref, left_ref, right_ref, sums, pad, patch, exits, ah, al, xh, xl, far, factor, num,
        grad, land_core, acc_core, density_sum, land_x, acc_x, land_ring, all_b,
        land_weight, land_edge, land_down, folded, land_beside,
        s_in, s_probe, r_probe, s_fwd, r_fwd, s_halo, r_halo, s_weight, r_weight, s_down, r_down, s_beside, r_beside,
        s_core, r_core, s_density, r_density, s_x, r_x, s_ring, r_ring, s_all, r_all,
        s_gather, r_gather,
    ):
        s = lax.axis_index("scan")
        m = lax.axis_index("mode")
        core = lax.rem(s, CORES)
        chip = lax.div(s, CORES)
        y, z = lax.rem(chip, side), lax.div(chip, side)
        other = (s + 1 - 2 * core, m)

        def near(ds, dm):
            return (lax.rem(s + ds + n_scan, n_scan), lax.rem(m + dm + n_mode, n_mode))

        ring_y = [((z * side + lax.rem(y + d, side)) * CORES + core, m) for d in range(1, side)]
        ring_z = [((lax.rem(z + d, side) * side + y) * CORES + core, m) for d in range(1, side)]
        peers_x = [near(0, d) for d in range(1, n_mode)]
        halo_steps = [(1, 0), (2, 0), (0, 1), (1, 1), (2, 1)]
        before = [near(-ds, -dm) for ds, dm in halo_steps]
        after = [near(ds, dm) for ds, dm in halo_steps]
        peers = [other] + ring_y + ring_z + peers_x + before + after

        started = []
        settled = []

        def settle(upto):
            while len(settled) < upto:
                started[len(settled)].wait_send()
                settled.append(True)

        def send(src, dst, send_sem, recv_sem, device):
            copy = pltpu.make_async_remote_copy(
                src_ref=src, dst_ref=dst, send_sem=send_sem, recv_sem=recv_sem,
                device_id=device, device_id_type=MESH,
            )
            copy.start()
            started.append(copy)
            return copy

        barrier = pltpu.get_barrier_semaphore()
        for device in peers:
            pl.semaphore_signal(barrier, inc=1, device_id=device, device_id_type=MESH)

        fetched = [
            pltpu.make_async_copy(obj_hbm.at[:, :, pl.ds(0, N)], ext.at[0, :, 0, pl.ds(0, tile), :], s_in.at[0]),
            pltpu.make_async_copy(obj_hbm.at[:, :, pl.ds(N, N)], ext.at[0, :, 1, pl.ds(0, tile), :], s_in.at[1]),
            pltpu.make_async_copy(probe_hbm.at[0], probes.at[0, pl.ds(2 * m, 2)], s_in.at[2]),
            pltpu.make_async_copy(right_hbm, right_ref, s_in.at[3]),
            pltpu.make_async_copy(left_hbm, left_ref, s_in.at[4]),
            pltpu.make_async_copy(amp_hbm, amp_ref, s_in.at[5]),
        ]
        for copy in fetched:
            copy.start()
        for copy in fetched[:3]:
            copy.wait()
        pl.semaphore_wait(barrier, len(peers))

        def start_halo(it):
            copies = []
            for i in (1, 2):
                copies.append(
                    send(ext.at[it, :, pl.ds(0, 2), pl.ds(0, tile), :],
                         ext.at[it, :, pl.ds(0, 2), pl.ds(i * tile, tile), :],
                         s_halo.at[it, i - 1], r_halo.at[it, i - 1], before[i - 1])
                )
            for i in range(3):
                copies.append(
                    send(ext.at[it, :, 0, pl.ds(0, tile), :],
                         ext.at[it, :, 2, pl.ds(i * tile, tile), :],
                         s_halo.at[it, 2 + i], r_halo.at[it, 2 + i], before[2 + i])
                )
            return copies

        mine = pl.ds(core * half, half)
        theirs = pl.ds((1 - core) * half, half)
        own_mode = pl.ds(2 * m, 2)
        arrival = [d for d in range(1, n_mode) if d != n_mode // 2] + [n_mode // 2]

        pairs = side // 2
        wide = 2 * rows

        def flipped(value, mask):
            out, bit = value, 1
            while bit <= mask:
                if mask & bit:
                    out = out + bit - 2 * bit * lax.rem(lax.div(value, bit), 2)
                bit *= 2
            return out

        far_first = sorted(range(pairs), key=lambda e: (e != pairs // 2, e == 0, e))

        def ring_of(it):
            return y * core + z * (1 - core) if SPLIT_RINGS[it] else z

        def block_of(it):
            return lax.div(ring_of(it), 2)

        def mode_of(d):
            return lax.rem(m - d + n_mode, n_mode)

        def send_mode(it, e, where):
            piece = probes.at[it, own_mode, where, :]
            return {d: send(piece, piece, s_probe.at[it, d, e], r_probe.at[it, d, e], near(0, d)) for d in arrival[::-1]}

        def trade(it, d):
            piece = probes.at[it, pl.ds(2 * mode_of(d), 2), mine, :]
            return send(piece, piece, s_fwd.at[it, d], r_fwd.at[it, d], other)

        probe_copies = [send_mode(0, 0, mine)]
        halo_copies = start_halo(0)
        trades = {}
        zero_half = jnp.zeros((64, N), F32)
        zero_block = jnp.zeros((256, N), F32)
        for j in range(2):
            for p in range(3):
                pad[j, p, 0] = zero_block
                pad[j, p, 3] = zero_block
                for c in (1, 2):
                    pad[j, p, c, 0:64, :] = zero_half
                    pad[j, p, c, 192:256, :] = zero_half

        lane = lax.broadcasted_iota(jnp.int32, (N, N), 1)
        row_id = lax.broadcasted_iota(jnp.int32, (N, N), 0)

        def used_of(j):
            return jnp.where(j < cnt_ref[0], 1.0, 0.0).astype(F32)

        def spot_of(j):
            row, col = lax.rem(off_ref[j, 0], tile), lax.rem(off_ref[j, 1], 2 * N)
            return row, lax.div(col, N), lax.rem(col, N)

        def take_patches(it):
            density = jnp.zeros((N, N), F32)
            for j in range(2):
                row, col_block, col_lane = spot_of(j)
                inside = (row_id + off_ref[j, 0] < far_rows) & (lane + off_ref[j, 1] < far_cols)
                for p in range(2):
                    one = ext[it, p, col_block, pl.ds(row, N), :]
                    two = ext[it, p, col_block + 1, pl.ds(row, N), :]
                    moved = pltpu.roll(jnp.where(lane >= col_lane, one, two), lax.rem(N - col_lane, N), 1)
                    moved = jnp.where(inside, moved, 0.0)
                    patch[j, p] = moved
                    density = density + moved * moved * used_of(j)
            grad[it, planes] = density

        def forward(it, d):
            k = mode_of(d)
            pr, pi = probes[it, 2 * k], probes[it, 2 * k + 1]
            for j in range(2):
                rows_j = pl.ds(j * N, N)
                o_re, o_im = patch[j, 0], patch[j, 1]
                for c, value in ((0, pr * o_re - pi * o_im), (1, pr * o_im + pi * o_re)):
                    cols_c = pl.ds(c * N, N)
                    exits[d, rows_j, cols_c] = value
                    high, low = split(value)
                    ah[d, rows_j, cols_c] = high
                    al[d, rows_j, cols_c] = low
            high, low = split(dot3(ah[d], al[d], right_ref[0], right_ref[1]))
            for j in range(2):
                for c in range(2):
                    block = (slice(j * N, (j + 1) * N), slice(c * N, (c + 1) * N))
                    xh[d, pl.ds(c * N, N), pl.ds(j * N, N)] = high[block]
                    xl[d, pl.ds(c * N, N), pl.ds(j * N, N)] = low[block]
            far[d] = dot3(left_ref[0], left_ref[1], xh[d], xl[d])

        def set_factors():
            for j in range(2):
                intensity = jnp.zeros((N, N), F32)
                for d in range(n_mode):
                    for c in range(2):
                        part = far[d, pl.ds(c * N, N), pl.ds(j * N, N)]
                        intensity = intensity + part * part
                factor[j] = amp_ref[j] / jnp.sqrt(jnp.maximum(intensity, 1.0))

        def backward(it, d, first):
            k = mode_of(d)
            for j in range(2):
                for c in range(2):
                    block = (pl.ds(c * N, N), pl.ds(j * N, N))
                    high, low = split(far[(d,) + block] * factor[j])
                    xh[(d,) + block] = high
                    xl[(d,) + block] = low
            high, low = split(dot3(right_ref[0], right_ref[1], xh[d], xl[d]))
            for j in range(2):
                for c in range(2):
                    block = (slice(c * N, (c + 1) * N), slice(j * N, (j + 1) * N))
                    ah[d, pl.ds(j * N, N), pl.ds(c * N, N)] = high[block]
                    al[d, pl.ds(j * N, N), pl.ds(c * N, N)] = low[block]
            change = dot3(ah[d], al[d], left_ref[0], left_ref[1]) - exits[d]
            pr, pi = probes[it, 2 * k], probes[it, 2 * k + 1]
            g_re = jnp.zeros((N, N), F32)
            g_im = jnp.zeros((N, N), F32)
            for j in range(2):
                c_re = change[j * N : (j + 1) * N, 0:N]
                c_im = change[j * N : (j + 1) * N, N : 2 * N]
                o_re, o_im = patch[j, 0] * used_of(j), patch[j, 1] * used_of(j)
                g_re = g_re + (o_re * c_re + o_im * c_im)
                g_im = g_im + (o_re * c_im - o_im * c_re)
                n_re = pr * c_re + pi * c_im
                n_im = pr * c_im - pi * c_re
                if first:
                    num[j, 0] = n_re
                    num[j, 1] = n_im
                else:
                    num[j, 0] += n_re
                    num[j, 1] += n_im
            grad[it, 2 * k] = g_re
            grad[it, 2 * k + 1] = g_im

        def set_pad(j, p, value):
            _, _, col_lane = spot_of(j)
            moved = pltpu.roll(value * used_of(j), col_lane, 1)
            pad[j, p, 1, 64:192, :] = jnp.where(lane >= col_lane, moved, 0.0)
            pad[j, p, 2, 64:192, :] = jnp.where(lane < col_lane, moved, 0.0)

        def placed(p, c):
            row_0, block_0, _ = spot_of(0)
            row_1, block_1, _ = spot_of(1)
            return (
                pad[0, p, c + 1 - block_0, pl.ds(64 - row_0, 192), :]
                + pad[1, p, c + 1 - block_1, pl.ds(64 - row_1, 192), :]
            )

        def weight_down(it):
            weight = jnp.zeros((N, N), F32)
            for p in range(planes):
                weight = weight + probes[it, p] * probes[it, p]
            for j in range(2):
                set_pad(j, 2, weight)
            for c in range(3):
                sums[it, c, 2] = placed(2, c)
            return [
                send(sums.at[it, :, 2, pl.ds(i * tile, tile), :], land_weight.at[it, i - 1],
                     s_weight.at[it, i - 1], r_weight.at[it, i - 1], after[i - 1])
                for i in (1, 2)
            ]

        def terms_down(it):
            for j in range(2):
                for p in range(2):
                    set_pad(j, p, num[j, p])
            copies = []
            for p in range(2):
                sums[it, 2, p] = placed(p, 2)
            for i in (1, 2):
                copies.append(
                    send(sums.at[it, 2, pl.ds(0, 2), pl.ds(i * tile, tile), :], land_edge.at[it, i - 1],
                         s_down.at[it, i - 1], r_down.at[it, i - 1], after[i - 1])
                )
            for c in range(2):
                for p in range(2):
                    sums[it, c, p] = placed(p, c)
            for i in (1, 2):
                copies.append(
                    send(sums.at[it, pl.ds(0, 2), pl.ds(0, 2), pl.ds(i * tile, tile), :], land_down.at[it, i - 1],
                         s_down.at[it, i + 1], r_down.at[it, i + 1], after[i - 1])
                )
            return copies

        def waves(it, halo_copies, mode_copies, trades):
            core_copies = {}

            def to_core(d, what):
                core_copies[d] = send(
                    grad.at[it, what, theirs, :], land_core.at[it, what], s_core.at[it, d], r_core.at[it, d], other
                )

            def pass_on(d):
                if d not in trades:
                    for copies in mode_copies:
                        copies[d].wait_recv()
                    trades[d] = trade(it, d)

            if it == 0:
                for d in arrival:
                    pass_on(d)
            for copy in halo_copies:
                copy.wait_recv()
            take_patches(it)
            to_core(n_mode, pl.ds(planes, 1))
            if 0 in trades:
                trades[0].wait_recv()
            forward(it, 0)
            for i, d in enumerate(arrival):
                pass_on(d)
                if i + 1 < len(arrival):
                    pass_on(arrival[i + 1])
                trades[d].wait_recv()
                forward(it, d)
            core_copies[n_mode].wait_recv()
            density_sum[it, 0] = grad[it, planes, mine, :] + land_core[it, planes]
            mode_sums = {}
            for d in range(1, n_mode):
                mode_sums[d] = send(density_sum.at[it, 0], density_sum.at[it, d],
                                    s_density.at[it, d - 1], r_density.at[it, d - 1], near(0, d))
            set_factors()
            down = weight_down(it)

            def fold(d):
                k = mode_of(d)
                core_copies[d].wait_recv()
                for c in range(2):
                    acc_core[it, k, c] = grad[it, 2 * k + c, mine, :] + land_core[it, 2 * k + c]
                if d > 0:
                    for e in far_first:
                        where = pl.ds(pl.multiple_of(flipped(block_of(it), e) * wide, wide), wide)
                        mode_sums[d, e] = send(
                            acc_core.at[it, k, :, where, :], land_x.at[it, d - 1, :, where, :],
                            s_x.at[it, d - 1, e], r_x.at[it, d - 1, e], near(0, n_mode - d),
                        )

            order = arrival[::-1] + [0]
            for i, d in enumerate(order):
                backward(it, d, i == 0)
                to_core(d, pl.ds(2 * mode_of(d), 2))
                if i > 0:
                    fold(order[i - 1])
            down = down + terms_down(it)
            fold(0)
            return mode_sums, down

        def reduce_steps(it, mode_sums, mode_copies, trades):
            last = it == ITERS - 1
            split_rings = SPLIT_RINGS[it]
            a = ring_of(it)
            b = y + z - a

            def at(first, second):
                if split_rings:
                    yy = second * (1 - core) + first * core
                    zz = first * (1 - core) + second * core
                else:
                    yy, zz = second, first
                return ((zz * side + yy) * CORES + core, m)

            peers_b = [at(a, lax.rem(b + d, side)) for d in range(1, side)]
            ring = {}
            total = density_sum[it, 0]
            for d in range(1, n_mode):
                mode_sums[d].wait_recv()
                total = total + density_sum[it, d]
            acc_x[it, 2] = total
            for e in far_first:
                where = pl.ds(pl.multiple_of(flipped(block_of(it), e) * wide, wide), wide)
                for d in range(1, n_mode):
                    mode_sums[d, e].wait_recv()
                for c in range(2):
                    total = acc_core[it, m, c, where, :]
                    for d in range(1, n_mode):
                        total = total + land_x[it, d - 1, c, where, :]
                    acc_x[it, c, where, :] = total
                for g in (2 * e, 2 * e + 1):
                    if g > 0:
                        t = flipped(a, g)
                        ring[g] = send(
                            acc_x.at[it, :, pl.ds(pl.multiple_of(t * rows, rows), rows), :], land_ring.at[it, g - 1],
                            s_ring.at[it, g - 1], r_ring.at[it, g - 1], at(t, b),
                        )
            yield
            total = acc_x[it, :, pl.ds(pl.multiple_of(a * rows, rows), rows), :]
            for g in range(1, side):
                ring[g].wait_recv()
                total = total + land_ring[it, g - 1]
            all_b[it, b] = total
            copies = [
                send(all_b.at[it, b], all_b.at[it, b], s_all.at[it, i], r_all.at[it, i], device)
                for i, device in enumerate(peers_b)
            ]
            yield
            for copy in copies:
                copy.wait_recv()
            total = all_b[it, 0]
            for i in range(1, side):
                total = total + all_b[it, i]
            spot = pl.ds(pl.multiple_of(core * half + a * rows, rows), rows)
            probes[it + 1, own_mode, spot, :] = probes[it, own_mode, spot, :] + total[0:2] / (total[2:3] + 1.0)
            piece = probes.at[it + 1, own_mode, spot, :]
            ring = {
                g: send(piece, piece, s_gather.at[it, g - 1], r_gather.at[it, g - 1], at(flipped(a, g), b))
                for g in range(side - 1, 0, -1)
            }
            yield
            for e in sorted(range(pairs), key=lambda e: (e == pairs // 2 and e > 0, e)):
                for g in (2 * e, 2 * e + 1):
                    if g > 0:
                        ring[g].wait_recv()
                if not last:
                    first_row = core * half + flipped(block_of(it), e) * wide
                    mode_copies.append(send_mode(it + 1, e, pl.ds(pl.multiple_of(first_row, wide), wide)))
            trades[0] = trade(it + 1, 0)
            if last:
                trades[0].wait_recv()
            yield

        def with_above(it, own, landed):
            for i in range(2):
                own = own + jnp.where(s > i, landed(i), 0.0)
            return own

        def weight_beside(it, down):
            for copy in down[:2]:
                copy.wait_recv()
            for c in range(3):
                folded[it, c, 2] = with_above(it, sums[it, c, 2, 0:tile, :], lambda i: land_weight[it, i, c])
            return send(folded.at[it, 2, 2], land_beside.at[it, 2], s_beside.at[it, 0], r_beside.at[it, 0], after[2])

        def terms_beside(it, down):
            for copy in down[2:4]:
                copy.wait_recv()
            for p in range(2):
                folded[it, 2, p] = with_above(it, sums[it, 2, p, 0:tile, :], lambda i: land_edge[it, i, p])
            return send(folded.at[it, 2, pl.ds(0, 2)], land_beside.at[it, pl.ds(0, 2)],
                        s_beside.at[it, 1], r_beside.at[it, 1], after[2])

        def new_object(it, copies):
            for copy in copies:
                copy.wait_recv()
            for c in range(2):
                terms = []
                for p in range(3):
                    if p == 2:
                        term = folded[it, c, 2]
                    else:
                        term = with_above(it, sums[it, c, p, 0:tile, :], lambda i: land_down[it, i, c, p])
                    if c == 0:
                        term = term + jnp.where(m > 0, land_beside[it, p], 0.0)
                    terms.append(term)
                for p in range(2):
                    fresh = ext[it, p, c, 0:tile, :] + terms[p] / (terms[2] + 1.0)
                    if it == ITERS - 1:
                        obj_new[p, :, c * N : (c + 1) * N] = fresh
                    else:
                        ext[it + 1, p, c, 0:tile, :] = fresh

        for copy in fetched[3:]:
            copy.wait()
        out_copies = []
        for it in range(ITERS):
            early = len(started)
            mode_sums, down = waves(it, halo_copies, probe_copies, trades)
            probe_copies, trades = [], {}
            steps = reduce_steps(it, mode_sums, probe_copies, trades)
            beside = [weight_beside(it, down)]
            next(steps)
            beside.append(terms_beside(it, down))
            next(steps)
            if it + 1 < ITERS:
                new_object(it, beside + down[4:])
                halo_copies = start_halo(it + 1)
            next(steps)
            if it + 1 == ITERS:
                new_object(it, beside + down[4:])
            settle(early)
            if it == ITERS - 1:
                out_copies.append(pltpu.make_async_copy(obj_new, obj_out, s_in.at[0]))
                out_copies[0].start()
                settle(len(started) - 2 * side)
            next(steps)
        out_copies.append(pltpu.make_async_copy(probes.at[ITERS, own_mode], probe_out.at[0], s_in.at[1]))
        out_copies[1].start()
        settle(len(started))
        for copy in out_copies:
            copy.wait()

    return kernel


def scratch_of(plan):
    n_mode, side, tile = plan.n_mode, plan.side, plan.tile
    planes, half, rows = plan.planes, plan.half, plan.rows

    def vmem(*shape, kind=F32):
        return pltpu.VMEM(shape, kind)

    def sems(*shape):
        return [pltpu.SemaphoreType.DMA(shape), pltpu.SemaphoreType.DMA(shape)]

    return [
        vmem(2, tile, 2 * N),
        vmem(ITERS, 2, 3, 3 * tile, N),
        vmem(ITERS + 1, planes, N, N),
        vmem(2, N, N),
        vmem(2, 2 * N, 2 * N, kind=BF16),
        vmem(2, 2 * N, 2 * N, kind=BF16),
        vmem(ITERS, 3, 3, 3 * tile, N),
        vmem(2, 3, 4, 256, N),
        vmem(2, 2, N, N),
        vmem(n_mode, 2 * N, 2 * N),
        vmem(n_mode, 2 * N, 2 * N, kind=BF16),
        vmem(n_mode, 2 * N, 2 * N, kind=BF16),
        vmem(n_mode, 2 * N, 2 * N, kind=BF16),
        vmem(n_mode, 2 * N, 2 * N, kind=BF16),
        vmem(n_mode, 2 * N, 2 * N),
        vmem(2, N, N),
        vmem(2, 2, N, N),
        vmem(ITERS, planes + 1, N, N),
        vmem(ITERS, planes + 1, half, N),
        vmem(ITERS, n_mode, 2, half, N),
        vmem(ITERS, n_mode, half, N),
        vmem(ITERS, n_mode - 1, 2, half, N),
        vmem(ITERS, 3, half, N),
        vmem(ITERS, side - 1, 3, rows, N),
        vmem(ITERS, side, 3, rows, N),
        vmem(ITERS, 2, 3, tile, N),
        vmem(ITERS, 2, 2, tile, N),
        vmem(ITERS, 2, 2, 2, tile, N),
        vmem(ITERS, 3, 3, tile, N),
        vmem(ITERS, 3, tile, N),
        pltpu.SemaphoreType.DMA((6,)),
        *sems(ITERS, n_mode, side // 2),
        *sems(ITERS + 1, n_mode),
        *sems(ITERS, 5),
        *sems(ITERS, 2),
        *sems(ITERS, 4),
        *sems(ITERS, 2),
        *sems(ITERS, n_mode + 1),
        *sems(ITERS, n_mode - 1),
        *sems(ITERS, n_mode - 1, side // 2),
        *sems(ITERS, side - 1),
        *sems(ITERS, side - 1),
        *sems(ITERS, side - 1),
    ]


def solution(mesh):
    n_scan, n_mode = mesh.shape["scan"], mesh.shape["mode"]
    left_np, right_np = fresnel_blocks()

    def local(object_field, probe, amplitude, offsets, counts):
        plan = Plan(n_scan, n_mode, object_field.shape[1])
        in_smem = pl.BlockSpec(memory_space=pltpu.SMEM)
        return pl.pallas_call(
            make_kernel(plan),
            out_shape=(
                jax.ShapeDtypeStruct(object_field.shape, F32),
                jax.ShapeDtypeStruct(probe.shape, F32),
            ),
            in_specs=[pl.BlockSpec(memory_space=pltpu.HBM)] * 5 + [in_smem] * 2,
            out_specs=(pl.BlockSpec(memory_space=pltpu.VMEM),) * 2,
            scratch_shapes=scratch_of(plan),
            compiler_params=pltpu.CompilerParams(
                collective_id=0, has_side_effects=True, vmem_limit_bytes=50 * 1024 * 1024
            ),
        )(
            *(
                pltpu.with_memory_space_constraint(value, pltpu.HBM)
                for value in (object_field, probe, amplitude, jnp.asarray(left_np), jnp.asarray(right_np))
            ),
            offsets,
            counts,
        )

    placed = (
        P(None, "scan", "mode"),
        P("mode", None, None, None),
        P(("scan", "mode"), None, None),
        P(("scan", "mode"), None),
        P(("scan", "mode")),
    )
    return jax.shard_map(
        local,
        mesh=mesh,
        in_specs=placed,
        out_specs=(P(None, "scan", "mode"), P("mode", None, None, None)),
        check_vma=False,
    )
```
